512 devices in a mesh: rows: 64 (over x, z), cols: 8 (over y, core).
Axes of the slice: x: 4, y: 4, z: 16, core: 2. Of those that a mesh axis runs over, the one named last changes fastest.
Arguments:
- residual: float32 [3, 4096, 8192], P(None, 'rows', 'cols'), may hold values from -6 to 6
- weights: float32 [3, 4096, 8192], P(None, 'rows', 'cols'), may hold values from 0.5 to 1.5
- accumulation: bfloat16 [3, 4096, 8192], P(None, 'rows', 'cols'), may hold values from 0.19921875 to 1
- mobility: bfloat16 [3, 4096, 8192], P(None, 'rows', 'cols'), may hold values from 0.099609375 to 1
- trans: float32 [4096, 8192], P('rows', 'cols'), may hold values from 0.05 to 2
- cell_inverse: bfloat16 [9, 4096, 8192], P(None, 'rows', 'cols'), may hold values from -2.390625 to 2.390625
- pressure_inverse: bfloat16 [64, 64, 128, 128], P('rows', 'cols'), may hold values from -0.5 to 0.5
- coarse_inverse: float32 [64, 8, 8, 8], P('rows', 'cols'), may hold values from -2 to 2
- intersection_counts: int32 [64, 2], P('rows'), may hold values from 1 to 32, as said below
- slot_map: int32 [256, 64], P('rows', 'cols'), may hold values from 0 to 63
Outputs:
- update: float32 [3, 4096, 8192], P(None, 'rows', 'cols')
The draws below stay inside these ranges and needn't reach their ends.
Inputs may be any that keep to these rules, and one draw needn't show every extreme that they name: `intersection_counts`: some entry equals 32 and some entry equals 1.
All inputs are finite; a program needn't handle non-finite values.
Results may differ from the reference program's by a relative error of at most 0.0017.
Values sent between devices are 32-bit elements; how exact they have to be, the bound alone decides.
A program may use at most 64 MiB of HBM per device.

```python
import math
import jax
import jax.numpy as jnp
from jax import lax

R_DEV = 64
H = 32
G = 128
PR = 16
PC = 128
KMAX = 8
E = 128
NR = 4096
NC = 8192
CB = 64
N_ROWS = 64
N_COLS = 8


def draw_intersection_counts(key, part):
    key_vals = jax.random.fold_in(key, 11)
    key_pos = jax.random.fold_in(key, 12)
    key_off = jax.random.fold_in(key, 13)
    values = jax.random.randint(key_vals, (N_ROWS * 2,), 1, H + 1).astype(jnp.int32)
    first = jax.random.randint(key_pos, (), 0, N_ROWS * 2).astype(jnp.int32)
    offset = jax.random.randint(key_off, (), 1, N_ROWS * 2).astype(jnp.int32)
    second = (first + offset) % (N_ROWS * 2)
    values = values.at[second].set(1)
    values = values.at[first].set(H)
    return values.reshape(N_ROWS, 2)


def touch_ends(result, key, least, high):
    spot = [jax.random.randint(jax.random.fold_in(key, axis), (), 0, length) for axis, length in enumerate(result.shape)]
    longest = result.shape.index(max(result.shape))
    neighbour = spot[:longest] + [(spot[longest] + 1) % result.shape[longest]] + spot[longest + 1:]
    return result.at[tuple(spot)].set(least).at[tuple(neighbour)].set(high)


def steps_of(stream_key, extent, cuts, smallest, high):
    loudness = 1.0
    for dim, shards_of in cuts:
        steps = jax.random.uniform(jax.random.fold_in(jax.random.fold_in(stream_key, 6), dim), (shards_of,), jnp.float32, smallest / len(cuts), high / len(cuts))
        loudness = loudness * jnp.repeat(jnp.exp(steps), extent[dim] // shards_of).reshape((-1,) + (1,) * (len(extent) - 1 - dim))
    return loudness


def normal_values(own_key, extent, scale, bound, pieces=(), held_as=jnp.bfloat16):
    factor_of = steps_of(own_key, extent, pieces, -0.22, 0.18) if pieces else 1.0
    result = jax.random.normal(own_key, extent, jnp.float32) * scale * factor_of
    return jnp.minimum(jnp.maximum(result, -bound), bound).astype(held_as)


def setup_inputs(seed: int = 0) -> dict:
    streams_of = jax.random.split(jax.random.key(seed), 11)
    return {
        "residual": normal_values(streams_of[0], (3, NR, NC), 1.0, 6.0, ((1, 64), (2, 8)), jnp.float32),
        "weights": jnp.clip(0.5 + 1.0 * jax.random.uniform(streams_of[1], (3, NR, NC), jnp.float32) ** steps_of(streams_of[1], (3, NR, NC), ((1, 64), (2, 8)), -0.2, 0.2), 0.5, 1.5),
        "accumulation": jnp.clip(0.19921875 + 0.80078125 * jax.random.uniform(streams_of[2], (3, NR, NC), jnp.float32) ** steps_of(streams_of[2], (3, NR, NC), ((1, 64), (2, 8)), -0.2, 0.2), 0.19921875, 1.0).astype(jnp.bfloat16),
        "mobility": jnp.clip(jnp.exp(math.log(1.0) - 2.306499 * jax.random.uniform(streams_of[3], (3, NR, NC), jnp.float32) ** steps_of(streams_of[3], (3, NR, NC), ((1, 64), (2, 8)), -0.2, 0.2)), 0.099609375, 1.0).astype(jnp.bfloat16),
        "trans": jnp.clip(jnp.exp(math.log(2.0) - 3.6888794 * jax.random.uniform(streams_of[4], (NR, NC), jnp.float32) ** steps_of(streams_of[4], (NR, NC), ((0, 64), (1, 8)), -0.2, 0.2)), 0.05, 2.0),
        "cell_inverse": normal_values(streams_of[5], (9, NR, NC), 0.4, 2.390625, ((1, 64), (2, 8))),
        "pressure_inverse": normal_values(streams_of[6], (N_ROWS, CB, E, E), E ** -0.5, 0.5, ((0, 64), (1, 8))),
        "coarse_inverse": normal_values(streams_of[7], (N_ROWS, N_COLS, KMAX, KMAX), KMAX ** -0.5, 2.0, ((0, 64), (1, 8)), jnp.float32),
        "intersection_counts": draw_intersection_counts(jax.random.fold_in(streams_of[10], 71), 0),
        "slot_map": touch_ends(jax.random.randint(streams_of[9], (NR // PR, NC // PC), 0, N_COLS * KMAX), jax.random.fold_in(streams_of[9], 1), 0, (N_COLS * KMAX) - 1).astype(jnp.int32),
    }


def reference(residual, weights, accumulation, mobility, trans, cell_inverse, pressure_inverse, coarse_inverse, intersection_counts, slot_map):
    hp = lax.Precision.HIGHEST
    rp = lax.optimization_barrier(jnp.sum(residual * weights, axis=0))
    padded = jnp.pad(rp, ((H, H), (0, 0)))
    e_index = jnp.arange(E, dtype=jnp.int32)
    sub_index = jnp.arange(N_ROWS, dtype=jnp.int32)

    def local(items):
        sub, inverse, counts = items
        block = lax.dynamic_slice_in_dim(padded, (sub * R_DEV).astype(jnp.int32), E, 0)
        keep = ((e_index >= H - counts[0]) & (e_index < R_DEV + H + counts[1])).astype(jnp.float32)
        ext = (block * keep[:, None]).astype(jnp.bfloat16)
        out = jnp.einsum('bij,jbg->ibg', inverse.astype(jnp.float32), ext.reshape(E, CB, G).astype(jnp.float32))
        return out.reshape(E, NC)[H:H + R_DEV]
    z_part = lax.map(local, (sub_index, pressure_inverse, intersection_counts)).reshape(NR, NC)
    npr = NR // PR
    npc = NC // PC
    slots = N_COLS * KMAX
    psum = rp.reshape(npr, PR, npc, PC).sum(axis=(1, 3)) * (1.0 / math.sqrt(PR * PC))
    onehot = (slot_map[:, :, None] == jnp.arange(slots, dtype=jnp.int32)).astype(jnp.float32)
    onehot = onehot.reshape(N_ROWS, R_DEV // PR, npc, slots)
    tiles = jnp.einsum('spq,spqk->sk', psum.reshape(N_ROWS, R_DEV // PR, npc), onehot, precision=hp)
    coarse = jnp.einsum('sokj,soj->sok', coarse_inverse, tiles.reshape(N_ROWS, N_COLS, KMAX), precision=hp).reshape(N_ROWS, slots)
    patch_corr = jnp.einsum('spqk,sk->spq', onehot, coarse, precision=hp).reshape(npr, npc)
    cell_corr = jnp.broadcast_to(patch_corr[:, None, :, None], (npr, PR, npc, PC)).reshape(NR, NC)
    dp = z_part + cell_corr
    tpad = jnp.pad(trans, 1)
    dpad = jnp.pad(dp, 1)
    flux = jnp.zeros((NR, NC), jnp.float32)
    for near_t, near_d in ((tpad[2:, 1:-1], dpad[2:, 1:-1]), (tpad[:-2, 1:-1], dpad[:-2, 1:-1]), (tpad[1:-1, 2:], dpad[1:-1, 2:]), (tpad[1:-1, :-2], dpad[1:-1, :-2])):
        flux = flux + 2.0 * trans * near_t / (trans + near_t) * (dp - near_d)
    r_two = residual - (accumulation.astype(jnp.float32) * dp[None] + mobility.astype(jnp.float32) * flux[None])
    blocks = cell_inverse.astype(jnp.float32).reshape(3, 3, NR, NC)
    update = lax.optimization_barrier(jnp.sum(blocks * r_two[None], axis=1))
    update = update.at[0].add(dp)
    return update
```

```python
import functools
import math

import jax
import jax.numpy as jnp
from jax import lax
from jax.experimental import pallas as pl
from jax.experimental.pallas import tpu as pltpu
from jax.sharding import PartitionSpec as P

H = 32
PR = 16
PC = 128
L = 128
TOP = 8
MESH = pl.DeviceIdType.MESH
F32 = jnp.float32
BF16 = jnp.bfloat16


def kernel(
    nr, nc,
    res_h, wts_h, acc_h, mob_h, trans_h, cell_h, pinv_h, ci_ref, cnt_ref, slot_ref,
    out_ref,
    res_v, wts_v, acc_v, mob_v, tp_v, cell_v, pinv_v,
    rp_v, halo_v, ext_v, trow_s, trow_r, tcol_r, drow_s, drow_r, dcol_r, dp_v, cv_v, ch_v,
    ps_v, tile_s, tile_r, corr_v,
    load_sem, send_sem, recv_sem, tile_send, tile_recv,
):
    rows = trans_h.shape[0]
    cols = trans_h.shape[1]
    nq = cols // L
    npr = rows // PR
    kmax = ci_ref.shape[-1]
    me_r = lax.axis_index("rows")
    me_c = lax.axis_index("cols")
    up = lax.rem(me_r + 1, nr)
    down = lax.rem(me_r + nr - 1, nr)
    right = lax.rem(me_c + 1, nc)
    left = lax.rem(me_c + nc - 1, nc)

    def load(src, dst, i):
        copy = pltpu.make_async_copy(src, dst, load_sem.at[i])
        copy.start()
        return copy

    rw = []
    for half in range(2):
        span = pl.ds(half * H, H)
        rw.append((
            load(res_h.at[:, span, :], res_v.at[:, span, :], 2 * half),
            load(wts_h.at[:, span, :], wts_v.at[:, span, :], 2 * half + 1),
        ))
    load_t = load(trans_h, tp_v.at[pl.ds(TOP, rows), :], 4)
    load_p = load(pinv_h.at[0], pinv_v, 5)
    load_a = load(acc_h, acc_v, 6)
    load_m = load(mob_h, mob_v, 7)
    load_c = load(cell_h, cell_v, 8)

    barrier = pltpu.get_barrier_semaphore()
    for target in (up, down):
        pl.semaphore_signal(barrier, inc=1, device_id=(target, me_c), device_id_type=MESH)
    for k in range(1, nc):
        pl.semaphore_signal(
            barrier, inc=1, device_id=(me_r, lax.rem(me_c + k, nc)), device_id_type=MESH
        )

    def send(src, dst, i, device):
        copy = pltpu.make_async_remote_copy(
            src_ref=src, dst_ref=dst, send_sem=send_sem.at[i], recv_sem=recv_sem.at[i],
            device_id=device, device_id_type=MESH,
        )
        copy.start()
        return copy

    lane8 = lax.broadcasted_iota(jnp.int32, (8, L), 1)
    block = jnp.zeros((kmax, L), F32)
    own = ci_ref[0, 0]
    for j in range(kmax):
        block = block + jnp.where(lane8 == me_c * kmax + j, own[:, j : j + 1], 0.0)
    tile_s[0:8, :] = block
    tile_s[8:16, :] = jnp.zeros((8, L), F32)

    row_e = lax.broadcasted_iota(jnp.int32, (H, L), 0)
    lo_count = jnp.where(me_r > 0, cnt_ref[0, 0], 0)
    hi_count = jnp.where(me_r < nr - 1, cnt_ref[0, 1], 0)

    halos = []
    for half in range(2):
        rw[half][0].wait()
        rw[half][1].wait()
        for p in range(half * H // PR, (half + 1) * H // PR):
            r = slice(p * PR, (p + 1) * PR)
            for q in range(nq):
                c = slice(q * L, (q + 1) * L)
                rp = res_v[0, r, c] * wts_v[0, r, c]
                rp = rp + res_v[1, r, c] * wts_v[1, r, c]
                rp = rp + res_v[2, r, c] * wts_v[2, r, c]
                rp_v[r, c] = rp
                ext_v[H + p * PR : H + (p + 1) * PR, c] = rp.astype(BF16)
                ps_v[p : p + 1, c] = jnp.sum(rp, axis=0, keepdims=True)
        if half == 0:
            pl.semaphore_wait(barrier, nc + 1)
            halos.append(send(rp_v.at[pl.ds(0, H), :], halo_v.at[1], 0, (down, me_c)))
        else:
            halos.append(send(rp_v.at[pl.ds(H, H), :], halo_v.at[0], 1, (up, me_c)))

    lane4 = lax.broadcasted_iota(jnp.int32, (npr, L), 1)
    slots = slot_ref[...]
    tiles = jnp.zeros((npr, L), F32)
    hot = []
    for q in range(nq):
        sums = jnp.sum(ps_v[0:npr, q * L : (q + 1) * L], axis=1, keepdims=True)
        hit = lane4 == slots[:, q : q + 1]
        hot.append(hit)
        tiles = tiles + jnp.where(hit, sums, 0.0)
    tiles = jnp.sum(tiles, axis=0, keepdims=True) * (1.0 / math.sqrt(PR * PC))
    tile_s[8:9, :] = tiles
    tile_copies = []
    for k in range(1, nc):
        copy = pltpu.make_async_remote_copy(
            src_ref=tile_s, dst_ref=tile_r.at[k],
            send_sem=tile_send.at[k], recv_sem=tile_recv.at[k],
            device_id=(me_r, lax.rem(me_c + k, nc)), device_id_type=MESH,
        )
        copy.start()
        tile_copies.append(copy)

    load_t.wait()
    trow_s[0] = tp_v[TOP : TOP + 1, :]
    trow_s[1] = tp_v[TOP + rows - 1 : TOP + rows, :]
    body = pl.ds(TOP, rows)
    first = pl.ds(0, L)
    last = pl.ds(cols - L, L)
    edge_t = [
        send(trow_s.at[0], trow_r.at[1], 2, (down, me_c)),
        send(trow_s.at[1], trow_r.at[0], 3, (up, me_c)),
        send(tp_v.at[body, first], tcol_r.at[1], 4, (me_r, left)),
        send(tp_v.at[body, last], tcol_r.at[0], 5, (me_r, right)),
    ]
    for copy in edge_t:
        copy.wait()
    tp_v[TOP - 1 : TOP, :] = trow_r[0]
    tp_v[TOP + rows : TOP + rows + 1, :] = trow_r[1]

    lane16 = lax.broadcasted_iota(jnp.int32, (PR, L), 1)
    is_last = lane16 == L - 1
    is_first = lane16 == 0

    def mean(a, b):
        return 2.0 * a * b / (a + b)

    for q in range(nq):
        c = slice(q * L, (q + 1) * L)
        low = mean(tp_v[TOP - 1 : TOP, c], tp_v[TOP : TOP + 1, c])
        cv_v[TOP - 1 : TOP, c] = jnp.where(me_r > 0, low, 0.0)
    for p in range(npr):
        r0 = TOP + p * PR
        blocks = [tcol_r[0, p * PR : (p + 1) * PR, :]]
        blocks += [tp_v[r0 : r0 + PR, q * L : (q + 1) * L] for q in range(nq)]
        blocks += [tcol_r[1, p * PR : (p + 1) * PR, :]]
        turned = [pltpu.roll(b, L - 1, 1) for b in blocks[1:]]
        for q in range(nq + 1):
            here = blocks[q]
            if q == 0:
                near = turned[0]
            else:
                near = jnp.where(is_last, turned[q], turned[q - 1])
            face = mean(here, near)
            if q == 0:
                face = jnp.where(me_c > 0, face, 0.0)
            if q == nq:
                face = jnp.where(is_last & (me_c == nc - 1), 0.0, face)
            ch_v[p * PR : (p + 1) * PR, q * L : (q + 1) * L] = face
            if q > 0:
                c = slice((q - 1) * L, q * L)
                cv_v[r0 : r0 + PR, c] = mean(here, tp_v[r0 + 1 : r0 + PR + 1, c])
    for q in range(nq):
        c = slice(q * L, (q + 1) * L)
        r = slice(TOP + rows - 1, TOP + rows)
        cv_v[r, c] = jnp.where(me_r < nr - 1, cv_v[r, c], 0.0)

    for copy in tile_copies:
        copy.wait()
    total = tile_s[8:16, :]
    for k in range(1, nc):
        total = total + tile_r[k, 8:16, :]
    total = total[0:1, :]
    sub8 = lax.broadcasted_iota(jnp.int32, (8, L), 0)
    coarse = jnp.zeros((8, L), F32)
    for k in range(nc):
        part = tile_s[0:8, :] if k == 0 else tile_r[k, 0:8, :]
        owner = lax.rem(me_c - k + nc, nc)
        value = jnp.sum(part * total, axis=1, keepdims=True)
        coarse = coarse + jnp.where(lane8 == owner * kmax + sub8, value, 0.0)
    coarse = jnp.sum(coarse, axis=0, keepdims=True)
    for q in range(nq):
        corr = jnp.sum(jnp.where(hot[q], coarse, 0.0), axis=1, keepdims=True)
        corr_v[0:npr, q * L : (q + 1) * L] = jnp.broadcast_to(corr, (npr, L))

    load_p.wait()
    for copy in halos:
        copy.wait()
    for q in range(nq):
        c = slice(q * L, (q + 1) * L)
        low = jnp.where(row_e >= H - lo_count, halo_v[0, :, c], 0.0)
        high = jnp.where(row_e < hi_count, halo_v[1, :, c], 0.0)
        ext_v[0:H, c] = low.astype(BF16)
        ext_v[H + rows : 2 * H + rows, c] = high.astype(BF16)
        z = jnp.dot(pinv_v[q, H : H + rows, :], ext_v[:, c], preferred_element_type=F32)
        for p in range(npr):
            dp = z[p * PR : (p + 1) * PR, :] + corr_v[p : p + 1, c]
            dp_v[TOP + p * PR : TOP + (p + 1) * PR, c] = dp
            if p == 0:
                drow_s[0, :, c] = dp[0:1, :]
            if p == npr - 1:
                drow_s[1, :, c] = dp[PR - 1 : PR, :]
    edge_d = [
        send(drow_s.at[0], drow_r.at[1], 6, (down, me_c)),
        send(drow_s.at[1], drow_r.at[0], 7, (up, me_c)),
        send(dp_v.at[body, first], dcol_r.at[1], 8, (me_r, left)),
        send(dp_v.at[body, last], dcol_r.at[0], 9, (me_r, right)),
    ]
    load_a.wait()
    load_m.wait()
    load_c.wait()
    for copy in edge_d:
        copy.wait()
    dp_v[TOP - 1 : TOP, :] = drow_r[0]
    dp_v[TOP + rows : TOP + rows + 1, :] = drow_r[1]

    for p in range(npr):
        r0 = TOP + p * PR
        r = slice(p * PR, (p + 1) * PR)
        blocks = [dcol_r[0, r, :]]
        blocks += [dp_v[r0 : r0 + PR, q * L : (q + 1) * L] for q in range(nq)]
        blocks += [dcol_r[1, r, :]]
        turned = [pltpu.roll(b, L - 1, 1) for b in blocks[1:]]
        before = None
        for q in range(nq + 1):
            here = blocks[q]
            if q == 0:
                near = turned[0]
            else:
                near = jnp.where(is_last, turned[q], turned[q - 1])
            face = ch_v[r, q * L : (q + 1) * L] * (here - near)
            moved = pltpu.roll(face, 1, 1)
            if q > 0:
                c = slice((q - 1) * L, q * L)
                flux = face - jnp.where(is_first, before, moved)
                flux = flux + cv_v[r0 : r0 + PR, c] * (here - dp_v[r0 + 1 : r0 + PR + 1, c])
                flux = flux + cv_v[r0 - 1 : r0 + PR - 1, c] * (here - dp_v[r0 - 1 : r0 + PR - 1, c])
                r2 = [
                    res_v[k, r, c]
                    - (acc_v[k, r, c].astype(F32) * here + mob_v[k, r, c].astype(F32) * flux)
                    for k in range(3)
                ]
                for k in range(3):
                    u = cell_v[3 * k, r, c].astype(F32) * r2[0]
                    u = u + cell_v[3 * k + 1, r, c].astype(F32) * r2[1]
                    u = u + cell_v[3 * k + 2, r, c].astype(F32) * r2[2]
                    if k == 0:
                        u = u + here
                    out_ref[k, r, c] = u
            before = moved


def shards(nr, nc, *args):
    residual, pinv = args[0], args[6]
    rows, cols = residual.shape[1:]
    groups = pinv.shape[1]
    e = rows + 2 * H
    hbm = pl.BlockSpec(memory_space=pl.ANY)
    vmem = pl.BlockSpec(memory_space=pltpu.VMEM)
    smem = pl.BlockSpec(memory_space=pltpu.SMEM)
    tall = rows + 2 * TOP
    scratch = [
        pltpu.VMEM((3, rows, cols), F32),
        pltpu.VMEM((3, rows, cols), F32),
        pltpu.VMEM((3, rows, cols), BF16),
        pltpu.VMEM((3, rows, cols), BF16),
        pltpu.VMEM((tall, cols), F32),
        pltpu.VMEM((9, rows, cols), BF16),
        pltpu.VMEM((groups, e, L), BF16),
        pltpu.VMEM((rows, cols), F32),
        pltpu.VMEM((2, H, cols), F32),
        pltpu.VMEM((e, cols), BF16),
        pltpu.VMEM((2, 1, cols), F32),
        pltpu.VMEM((2, 1, cols), F32),
        pltpu.VMEM((2, rows, L), F32),
        pltpu.VMEM((2, 1, cols), F32),
        pltpu.VMEM((2, 1, cols), F32),
        pltpu.VMEM((2, rows, L), F32),
        pltpu.VMEM((tall, cols), F32),
        pltpu.VMEM((tall, cols), F32),
        pltpu.VMEM((rows, cols + L), F32),
        pltpu.VMEM((8, cols), F32),
        pltpu.VMEM((16, L), F32),
        pltpu.VMEM((nc, 16, L), F32),
        pltpu.VMEM((8, cols), F32),
        pltpu.SemaphoreType.DMA((9,)),
        pltpu.SemaphoreType.DMA((10,)),
        pltpu.SemaphoreType.DMA((10,)),
        pltpu.SemaphoreType.DMA((nc,)),
        pltpu.SemaphoreType.DMA((nc,)),
    ]
    return pl.pallas_call(
        functools.partial(kernel, nr, nc),
        out_shape=jax.ShapeDtypeStruct((3, rows, cols), F32),
        in_specs=[hbm] * 7 + [vmem, smem, vmem],
        out_specs=vmem,
        scratch_shapes=scratch,
        compiler_params=pltpu.CompilerParams(
            collective_id=0, has_side_effects=True, vmem_limit_bytes=60 * 1024 * 1024
        ),
    )(*args)


def solution(mesh):
    in_specs = (
        P(None, "rows", "cols"),
        P(None, "rows", "cols"),
        P(None, "rows", "cols"),
        P(None, "rows", "cols"),
        P("rows", "cols"),
        P(None, "rows", "cols"),
        P("rows", "cols", None, None),
        P("rows", "cols", None, None),
        P("rows", None),
        P("rows", "cols"),
    )
    out_specs = P(None, "rows", "cols")
    body = functools.partial(shards, mesh.shape["rows"], mesh.shape["cols"])
    return jax.shard_map(body, mesh=mesh, in_specs=in_specs, out_specs=out_specs, check_vma=False)
```

```python
import functools
import math

import jax
import jax.numpy as jnp
from jax import lax
from jax.experimental import pallas as pl
from jax.experimental.pallas import tpu as pltpu
from jax.sharding import PartitionSpec as P

H = 32
PR = 16
PC = 128
L = 128
TOP = 8
MESH = pl.DeviceIdType.MESH
F32 = jnp.float32
BF16 = jnp.bfloat16


def kernel(
    nr, nc,
    res_h, wts_h, acc_h, mob_h, trans_h, cell_h, pinv_h, ci_h, cnt_h, slot_h,
    out_ref,
    res_v, wts_v, acc_v, mob_v, tp_v, cell_v, pinv_v, ci_v, cnt_s, slot_v,
    rp_v, halo_v, ext_v, trow_s, trow_r, tcol_r, drow_s, drow_r, dcol_r, dp_v, cv_v, chr_v, chl_v,
    ps_v, tile_s, tile_r, corr_v,
    load_sem, send_sem, recv_sem, tile_send, tile_recv,
):
    rows = trans_h.shape[0]
    cols = trans_h.shape[1]
    nq = cols // L
    npr = rows // PR
    kmax = ci_h.shape[-1]
    pairs = nq // 2
    order = [pairs - 1] + list(range(pairs - 1))
    me_r = lax.axis_index("rows")
    me_c = lax.axis_index("cols")
    up = lax.rem(me_r + 1, nr)
    down = lax.rem(me_r + nr - 1, nr)
    right = lax.rem(me_c + 1, nc)
    left = lax.rem(me_c + nc - 1, nc)

    def load(src, dst, i):
        copy = pltpu.make_async_copy(src, dst, load_sem.at[i])
        copy.start()
        return copy

    rw = []
    for n, w in enumerate(order):
        span = pl.ds(w * 2 * L, 2 * L)
        rw.append((
            load(res_h.at[:, :, span], res_v.at[:, :, span], 2 * n),
            load(wts_h.at[:, :, span], wts_v.at[:, :, span], 2 * n + 1),
        ))
        if n == 0:
            load_t = load(trans_h, tp_v.at[pl.ds(TOP, rows), :], 8)
            load_ci = load(ci_h.at[0, 0], ci_v, 9)
            load_slot = load(slot_h, slot_v, 10)
            load_cnt = load(cnt_h, cnt_s, 11)
    load_p = load(pinv_h.at[0], pinv_v, 12)
    load_m = load(mob_h, mob_v, 13)
    load_a = load(acc_h, acc_v, 14)
    load_c = load(cell_h, cell_v, 15)

    barrier = pltpu.get_barrier_semaphore()
    for target in (up, down):
        pl.semaphore_signal(barrier, inc=1, device_id=(target, me_c), device_id_type=MESH)
    for k in range(1, nc):
        pl.semaphore_signal(
            barrier, inc=1, device_id=(me_r, lax.rem(me_c + k, nc)), device_id_type=MESH
        )

    sent = []

    def send(src, dst, i, device):
        copy = pltpu.make_async_remote_copy(
            src_ref=src, dst_ref=dst, send_sem=send_sem.at[i], recv_sem=recv_sem.at[i],
            device_id=device, device_id_type=MESH,
        )
        copy.start()
        sent.append(copy)
        return copy

    body = pl.ds(TOP, rows)
    first = pl.ds(0, L)
    last = pl.ds(cols - L, L)
    halos = []
    for n, w in enumerate(order):
        rw[n][0].wait()
        rw[n][1].wait()
        for q in (2 * w, 2 * w + 1):
            c = slice(q * L, (q + 1) * L)
            for p in range(npr):
                r = slice(p * PR, (p + 1) * PR)
                rp = res_v[0, r, c] * wts_v[0, r, c]
                rp = rp + res_v[1, r, c] * wts_v[1, r, c]
                rp = rp + res_v[2, r, c] * wts_v[2, r, c]
                rp_v[r, c] = rp
                ext_v[H + p * PR : H + (p + 1) * PR, c] = rp.astype(BF16)
                ps_v[p : p + 1, c] = jnp.sum(rp, axis=0, keepdims=True)
        if n == 0:
            pl.semaphore_wait(barrier, nc + 1)
        span = pl.ds(w * 2 * L, 2 * L)
        halos.append((
            send(rp_v.at[pl.ds(0, H), span], halo_v.at[1, :, span], 2 * n, (down, me_c)),
            send(rp_v.at[pl.ds(H, H), span], halo_v.at[0, :, span], 2 * n + 1, (up, me_c)),
        ))
        if n == 0:
            load_t.wait()
            trow_s[0] = tp_v[TOP : TOP + 1, :]
            trow_s[1] = tp_v[TOP + rows - 1 : TOP + rows, :]
            edge_t = [
                send(tp_v.at[body, first], tcol_r.at[1], 8, (me_r, left)),
                send(tp_v.at[body, last], tcol_r.at[0], 9, (me_r, right)),
                send(trow_s.at[0], trow_r.at[1], 10, (down, me_c)),
                send(trow_s.at[1], trow_r.at[0], 11, (up, me_c)),
            ]

    load_ci.wait()
    load_slot.wait()
    lane8 = lax.broadcasted_iota(jnp.int32, (8, L), 1)
    sub8 = lax.broadcasted_iota(jnp.int32, (8, L), 0)
    block = jnp.zeros((kmax, L), F32)
    own = ci_v[...]
    for j in range(kmax):
        block = block + jnp.where(lane8 == me_c * kmax + j, own[:, j : j + 1], 0.0)
    tile_s[0:8, :] = block
    tile_s[8:16, :] = jnp.zeros((8, L), F32)
    lane4 = lax.broadcasted_iota(jnp.int32, (npr, L), 1)
    slots = slot_v[...]
    tiles = jnp.zeros((npr, L), F32)
    hot = []
    for q in range(nq):
        sums = jnp.sum(ps_v[0:npr, q * L : (q + 1) * L], axis=1, keepdims=True)
        hit = lane4 == slots[:, q : q + 1]
        hot.append(hit)
        tiles = tiles + jnp.where(hit, sums, 0.0)
    tiles = jnp.sum(tiles, axis=0, keepdims=True) * (1.0 / math.sqrt(PR * PC))
    tile_s[8:9, :] = tiles
    tile_copies = []
    for k in range(1, nc):
        copy = pltpu.make_async_remote_copy(
            src_ref=tile_s, dst_ref=tile_r.at[k],
            send_sem=tile_send.at[k], recv_sem=tile_recv.at[k],
            device_id=(me_r, lax.rem(me_c + k, nc)), device_id_type=MESH,
        )
        copy.start()
        tile_copies.append(copy)

    for copy in edge_t:
        copy.wait_recv()
    tp_v[TOP - 1 : TOP, :] = trow_r[0]
    tp_v[TOP + rows : TOP + rows + 1, :] = trow_r[1]

    lane16 = lax.broadcasted_iota(jnp.int32, (PR, L), 1)
    is_last = lane16 == L - 1
    is_first = lane16 == 0

    def mean(a, b):
        return 2.0 * a * b / (a + b)

    for q in range(nq):
        c = slice(q * L, (q + 1) * L)
        low = mean(tp_v[TOP - 1 : TOP, c], tp_v[TOP : TOP + 1, c])
        cv_v[TOP - 1 : TOP, c] = jnp.where(me_r > 0, low, 0.0)
    for p in range(npr):
        r0 = TOP + p * PR
        r = slice(p * PR, (p + 1) * PR)
        blocks = [tcol_r[0, r, :]]
        blocks += [tp_v[r0 : r0 + PR, q * L : (q + 1) * L] for q in range(nq)]
        blocks += [tcol_r[1, r, :]]
        turned = [pltpu.roll(b, L - 1, 1) for b in blocks[1:]]
        before = None
        for q in range(nq + 1):
            here = blocks[q]
            if q == 0:
                near = turned[0]
            else:
                near = jnp.where(is_last, turned[q], turned[q - 1])
            face = mean(here, near)
            if q == 0:
                face = jnp.where(me_c > 0, face, 0.0)
            if q == nq:
                face = jnp.where(is_last & (me_c == nc - 1), 0.0, face)
            moved = pltpu.roll(face, 1, 1)
            if q > 0:
                c = slice((q - 1) * L, q * L)
                chr_v[r, c] = face
                chl_v[r, c] = jnp.where(is_first, before, moved)
                cv_v[r0 : r0 + PR, c] = mean(here, tp_v[r0 + 1 : r0 + PR + 1, c])
            before = moved
    for q in range(nq):
        c = slice(q * L, (q + 1) * L)
        r = slice(TOP + rows - 1, TOP + rows)
        cv_v[r, c] = jnp.where(me_r < nr - 1, cv_v[r, c], 0.0)

    load_p.wait()
    load_cnt.wait()
    row_e = lax.broadcasted_iota(jnp.int32, (H, L), 0)
    lo_count = jnp.where(me_r > 0, cnt_s[0, 0], 0)
    hi_count = jnp.where(me_r < nr - 1, cnt_s[0, 1], 0)

    for copy in tile_copies:
        copy.wait_recv()
    total = tile_s[8:16, :]
    for k in range(1, nc):
        total = total + tile_r[k, 8:16, :]
    total = total[0:1, :]
    coarse = jnp.zeros((8, L), F32)
    for k in range(nc):
        part = tile_s[0:8, :] if k == 0 else tile_r[k, 0:8, :]
        owner = lax.rem(me_c - k + nc, nc)
        value = jnp.sum(part * total, axis=1, keepdims=True)
        coarse = coarse + jnp.where(lane8 == owner * kmax + sub8, value, 0.0)
    coarse = jnp.sum(coarse, axis=0, keepdims=True)
    for q in range(nq):
        corr = jnp.sum(jnp.where(hot[q], coarse, 0.0), axis=1, keepdims=True)
        corr_v[0:npr, q * L : (q + 1) * L] = jnp.broadcast_to(corr, (npr, L))

    edge_c = []
    edge_r = []
    for n, w in enumerate(order):
        for copy in halos[n]:
            copy.wait_recv()
        for q in (2 * w, 2 * w + 1):
            c = slice(q * L, (q + 1) * L)
            low = jnp.where(row_e >= H - lo_count, halo_v[0, :, c], 0.0)
            high = jnp.where(row_e < hi_count, halo_v[1, :, c], 0.0)
            ext_v[0:H, c] = low.astype(BF16)
            ext_v[H + rows : 2 * H + rows, c] = high.astype(BF16)
            z = jnp.dot(pinv_v[q, H : H + rows, :], ext_v[:, c], preferred_element_type=F32)
            for p in range(npr):
                dp = z[p * PR : (p + 1) * PR, :] + corr_v[p : p + 1, c]
                dp_v[TOP + p * PR : TOP + (p + 1) * PR, c] = dp
                if p == 0:
                    drow_s[0, :, c] = dp[0:1, :]
                    dp_v[TOP - 1 : TOP, c] = dp[0:1, :]
                if p == npr - 1:
                    drow_s[1, :, c] = dp[PR - 1 : PR, :]
                    dp_v[TOP + rows : TOP + rows + 1, c] = dp[PR - 1 : PR, :]
        span = pl.ds(w * 2 * L, 2 * L)
        edge_r.append(send(drow_s.at[0, :, span], drow_r.at[1, :, span], 12 + 2 * n, (down, me_c)))
        edge_r.append(send(drow_s.at[1, :, span], drow_r.at[0, :, span], 13 + 2 * n, (up, me_c)))
        if w == pairs - 1:
            edge_c.append(send(dp_v.at[body, last], dcol_r.at[0], 20, (me_r, right)))
        if w == 0:
            edge_c.append(send(dp_v.at[body, first], dcol_r.at[1], 21, (me_r, left)))

    load_m.wait()
    load_a.wait()
    load_c.wait()

    def column(p, q):
        r0 = TOP + p * PR
        if q < 0:
            return dcol_r[0, p * PR : (p + 1) * PR, :]
        if q == nq:
            return dcol_r[1, p * PR : (p + 1) * PR, :]
        return dp_v[r0 : r0 + PR, q * L : (q + 1) * L]

    def finish(p, q):
        r0 = TOP + p * PR
        r = slice(p * PR, (p + 1) * PR)
        c = slice(q * L, (q + 1) * L)
        here = column(p, q)
        after = jnp.where(is_last, pltpu.roll(column(p, q + 1), L - 1, 1), pltpu.roll(here, L - 1, 1))
        prior = jnp.where(is_first, pltpu.roll(column(p, q - 1), 1, 1), pltpu.roll(here, 1, 1))
        flux = chr_v[r, c] * (here - after) + chl_v[r, c] * (here - prior)
        flux = flux + cv_v[r0 : r0 + PR, c] * (here - dp_v[r0 + 1 : r0 + PR + 1, c])
        flux = flux + cv_v[r0 - 1 : r0 + PR - 1, c] * (here - dp_v[r0 - 1 : r0 + PR - 1, c])
        r2 = [
            res_v[k, r, c]
            - (acc_v[k, r, c].astype(F32) * here + mob_v[k, r, c].astype(F32) * flux)
            for k in range(3)
        ]
        for k in range(3):
            u = cell_v[3 * k, r, c].astype(F32) * r2[0]
            u = u + cell_v[3 * k + 1, r, c].astype(F32) * r2[1]
            u = u + cell_v[3 * k + 2, r, c].astype(F32) * r2[2]
            if k == 0:
                u = u + here
            out_ref[k, r, c] = u

    for q in range(1, nq - 1):
        for p in range(npr):
            finish(p, q)
    for copy in edge_c:
        copy.wait_recv()
    for q in (0, nq - 1):
        for p in range(npr):
            finish(p, q)
    for copy in edge_r:
        copy.wait_recv()
    for q in range(nq):
        c = slice(q * L, (q + 1) * L)
        for e in range(2):
            r = slice(0, 8) if e == 0 else slice(rows - 8, rows)
            face = slice(TOP - 1, TOP) if e == 0 else slice(TOP + rows - 1, TOP + rows)
            mine = slice(TOP, TOP + 1) if e == 0 else slice(TOP + rows - 1, TOP + rows)
            extra = cv_v[face, c] * (dp_v[mine, c] - drow_r[e, :, c])
            extra = jnp.where(sub8 == (0 if e == 0 else 7), extra, 0.0)
            m = [mob_v[j, r, c].astype(F32) * extra for j in range(3)]
            for k in range(3):
                u = cell_v[3 * k, r, c].astype(F32) * m[0]
                u = u + cell_v[3 * k + 1, r, c].astype(F32) * m[1]
                u = u + cell_v[3 * k + 2, r, c].astype(F32) * m[2]
                out_ref[k, r, c] = out_ref[k, r, c] - u
    for copy in sent + tile_copies:
        copy.wait_send()


def shards(nr, nc, *args):
    residual, pinv = args[0], args[6]
    rows, cols = residual.shape[1:]
    groups = pinv.shape[1]
    e = rows + 2 * H
    hbm = pl.BlockSpec(memory_space=pl.ANY)
    vmem = pl.BlockSpec(memory_space=pltpu.VMEM)
    tall = rows + 2 * TOP
    scratch = [
        pltpu.VMEM((3, rows, cols), F32),
        pltpu.VMEM((3, rows, cols), F32),
        pltpu.VMEM((3, rows, cols), BF16),
        pltpu.VMEM((3, rows, cols), BF16),
        pltpu.VMEM((tall, cols), F32),
        pltpu.VMEM((9, rows, cols), BF16),
        pltpu.VMEM((groups, e, L), BF16),
        pltpu.VMEM(args[7].shape[2:], F32),
        pltpu.SMEM(args[8].shape, jnp.int32),
        pltpu.VMEM(args[9].shape, jnp.int32),
        pltpu.VMEM((rows, cols), F32),
        pltpu.VMEM((2, H, cols), F32),
        pltpu.VMEM((e, cols), BF16),
        pltpu.VMEM((2, 1, cols), F32),
        pltpu.VMEM((2, 1, cols), F32),
        pltpu.VMEM((2, rows, L), F32),
        pltpu.VMEM((2, 1, cols), F32),
        pltpu.VMEM((2, 1, cols), F32),
        pltpu.VMEM((2, rows, L), F32),
        pltpu.VMEM((tall, cols), F32),
        pltpu.VMEM((tall, cols), F32),
        pltpu.VMEM((rows, cols), F32),
        pltpu.VMEM((rows, cols), F32),
        pltpu.VMEM((8, cols), F32),
        pltpu.VMEM((16, L), F32),
        pltpu.VMEM((nc, 16, L), F32),
        pltpu.VMEM((8, cols), F32),
        pltpu.SemaphoreType.DMA((16,)),
        pltpu.SemaphoreType.DMA((22,)),
        pltpu.SemaphoreType.DMA((22,)),
        pltpu.SemaphoreType.DMA((nc,)),
        pltpu.SemaphoreType.DMA((nc,)),
    ]
    return pl.pallas_call(
        functools.partial(kernel, nr, nc),
        out_shape=pltpu.VMEM((3, rows, cols), F32),
        in_specs=[hbm] * 10,
        out_specs=vmem,
        scratch_shapes=scratch,
        compiler_params=pltpu.CompilerParams(
            collective_id=0, has_side_effects=True, vmem_limit_bytes=60 * 1024 * 1024
        ),
    )(*args)


def solution(mesh):
    in_specs = (
        P(None, "rows", "cols"),
        P(None, "rows", "cols"),
        P(None, "rows", "cols"),
        P(None, "rows", "cols"),
        P("rows", "cols"),
        P(None, "rows", "cols"),
        P("rows", "cols", None, None),
        P("rows", "cols", None, None),
        P("rows", None),
        P("rows", "cols"),
    )
    out_specs = P(None, "rows", "cols")
    body = functools.partial(shards, mesh.shape["rows"], mesh.shape["cols"])
    return jax.shard_map(body, mesh=mesh, in_specs=in_specs, out_specs=out_specs, check_vma=False)
```

```python
import functools
import math

import jax
import jax.numpy as jnp
from jax import lax
from jax.experimental import pallas as pl
from jax.experimental.pallas import tpu as pltpu
from jax.sharding import PartitionSpec as P

H = 32
PR = 16
PC = 128
L = 128
TOP = 8
MESH = pl.DeviceIdType.MESH
F32 = jnp.float32
BF16 = jnp.bfloat16


def kernel(
    nr, nc,
    res_h, wts_h, acc_h, mob_h, trans_h, cell_h, pinv_h, ci_h, cnt_h, slot_h,
    out_ref,
    res_v, wts_v, acc_v, mob_v, tp_v, cell_v, pinv_v, ci_v, cnt_s, slot_v,
    rp_v, halo_v, ext_v, trow_s, trow_r, tcol_r, drow_s, drow_r, dcol_r, dp_v, cv_v, chr_v, chl_v,
    ps_v, tile_s, tile_r, corr_v,
    load_sem, send_sem, recv_sem, tile_send, tile_recv,
):
    rows = trans_h.shape[0]
    cols = trans_h.shape[1]
    nq = cols // L
    npr = rows // PR
    kmax = ci_h.shape[-1]
    pairs = nq // 2
    order = [pairs - 1] + list(range(pairs - 1))
    me_r = lax.axis_index("rows")
    me_c = lax.axis_index("cols")
    up = lax.rem(me_r + 1, nr)
    down = lax.rem(me_r + nr - 1, nr)
    right = lax.rem(me_c + 1, nc)
    left = lax.rem(me_c + nc - 1, nc)

    def load(src, dst, i):
        copy = pltpu.make_async_copy(src, dst, load_sem.at[i])
        copy.start()
        return copy

    rw = []
    for n, w in enumerate(order):
        span = pl.ds(w * 2 * L, 2 * L)
        rw.append((
            load(res_h.at[:, :, span], res_v.at[:, :, span], 2 * n),
            load(wts_h.at[:, :, span], wts_v.at[:, :, span], 2 * n + 1),
        ))
        if n == 0:
            load_t = load(trans_h, tp_v.at[pl.ds(TOP, rows), :], 8)
            load_ci = load(ci_h.at[0, 0], ci_v, 9)
            load_slot = load(slot_h, slot_v, 10)
            load_cnt = load(cnt_h, cnt_s, 11)
    barrier = pltpu.get_barrier_semaphore()
    for target in (up, down):
        pl.semaphore_signal(barrier, inc=1, device_id=(target, me_c), device_id_type=MESH)
    for k in range(1, nc):
        pl.semaphore_signal(
            barrier, inc=1, device_id=(me_r, lax.rem(me_c + k, nc)), device_id_type=MESH
        )

    sent = []

    def send(src, dst, i, device):
        copy = pltpu.make_async_remote_copy(
            src_ref=src, dst_ref=dst, send_sem=send_sem.at[i], recv_sem=recv_sem.at[i],
            device_id=device, device_id_type=MESH,
        )
        copy.start()
        sent.append(copy)
        return copy

    body = pl.ds(TOP, rows)
    first = pl.ds(0, L)
    last = pl.ds(cols - L, L)
    halos = []
    for n, w in enumerate(order):
        rw[n][0].wait()
        rw[n][1].wait()
        for q in (2 * w, 2 * w + 1):
            c = slice(q * L, (q + 1) * L)
            for p in range(npr):
                r = slice(p * PR, (p + 1) * PR)
                rp = res_v[0, r, c] * wts_v[0, r, c]
                rp = rp + res_v[1, r, c] * wts_v[1, r, c]
                rp = rp + res_v[2, r, c] * wts_v[2, r, c]
                rp_v[r, c] = rp
                ext_v[H + p * PR : H + (p + 1) * PR, c] = rp.astype(BF16)
                ps_v[p : p + 1, c] = jnp.sum(rp, axis=0, keepdims=True)
        if n == 0:
            pl.semaphore_wait(barrier, nc + 1)
        span = pl.ds(w * 2 * L, 2 * L)
        halos.append((
            send(rp_v.at[pl.ds(0, H), span], halo_v.at[1, :, span], 2 * n, (down, me_c)),
            send(rp_v.at[pl.ds(H, H), span], halo_v.at[0, :, span], 2 * n + 1, (up, me_c)),
        ))
        if n == 0:
            load_t.wait()
            trow_s[0] = tp_v[TOP : TOP + 1, :]
            trow_s[1] = tp_v[TOP + rows - 1 : TOP + rows, :]
            edge_t = [
                send(tp_v.at[body, first], tcol_r.at[1], 8, (me_r, left)),
                send(tp_v.at[body, last], tcol_r.at[0], 9, (me_r, right)),
                send(trow_s.at[0], trow_r.at[1], 10, (down, me_c)),
                send(trow_s.at[1], trow_r.at[0], 11, (up, me_c)),
            ]

    load_p = load(pinv_h.at[0], pinv_v, 12)
    load_m = load(mob_h, mob_v, 13)
    load_a = load(acc_h, acc_v, 14)
    load_c = load(cell_h, cell_v, 15)

    load_ci.wait()
    load_slot.wait()
    lane8 = lax.broadcasted_iota(jnp.int32, (8, L), 1)
    sub8 = lax.broadcasted_iota(jnp.int32, (8, L), 0)
    block = jnp.zeros((kmax, L), F32)
    own = ci_v[...]
    for j in range(kmax):
        block = block + jnp.where(lane8 == me_c * kmax + j, own[:, j : j + 1], 0.0)
    tile_s[0:8, :] = block
    tile_s[8:16, :] = jnp.zeros((8, L), F32)
    lane4 = lax.broadcasted_iota(jnp.int32, (npr, L), 1)
    slots = slot_v[...]
    tiles = jnp.zeros((npr, L), F32)
    hot = []
    for q in range(nq):
        sums = jnp.sum(ps_v[0:npr, q * L : (q + 1) * L], axis=1, keepdims=True)
        hit = lane4 == slots[:, q : q + 1]
        hot.append(hit)
        tiles = tiles + jnp.where(hit, sums, 0.0)
    tiles = jnp.sum(tiles, axis=0, keepdims=True) * (1.0 / math.sqrt(PR * PC))
    tile_s[8:9, :] = tiles
    tile_copies = []
    for k in range(1, nc):
        copy = pltpu.make_async_remote_copy(
            src_ref=tile_s, dst_ref=tile_r.at[k],
            send_sem=tile_send.at[k], recv_sem=tile_recv.at[k],
            device_id=(me_r, lax.rem(me_c + k, nc)), device_id_type=MESH,
        )
        copy.start()
        tile_copies.append(copy)

    for copy in edge_t:
        copy.wait_recv()
    tp_v[TOP - 1 : TOP, :] = trow_r[0]
    tp_v[TOP + rows : TOP + rows + 1, :] = trow_r[1]

    lane16 = lax.broadcasted_iota(jnp.int32, (PR, L), 1)
    is_last = lane16 == L - 1
    is_first = lane16 == 0

    def mean(a, b):
        return 2.0 * a * b / (a + b)

    for q in range(nq):
        c = slice(q * L, (q + 1) * L)
        low = mean(tp_v[TOP - 1 : TOP, c], tp_v[TOP : TOP + 1, c])
        cv_v[TOP - 1 : TOP, c] = jnp.where(me_r > 0, low, 0.0)
    for p in range(npr):
        r0 = TOP + p * PR
        r = slice(p * PR, (p + 1) * PR)
        blocks = [tcol_r[0, r, :]]
        blocks += [tp_v[r0 : r0 + PR, q * L : (q + 1) * L] for q in range(nq)]
        blocks += [tcol_r[1, r, :]]
        turned = [pltpu.roll(b, L - 1, 1) for b in blocks[1:]]
        before = None
        for q in range(nq + 1):
            here = blocks[q]
            if q == 0:
                near = turned[0]
            else:
                near = jnp.where(is_last, turned[q], turned[q - 1])
            face = mean(here, near)
            if q == 0:
                face = jnp.where(me_c > 0, face, 0.0)
            if q == nq:
                face = jnp.where(is_last & (me_c == nc - 1), 0.0, face)
            moved = pltpu.roll(face, 1, 1)
            if q > 0:
                c = slice((q - 1) * L, q * L)
                chr_v[r, c] = face
                chl_v[r, c] = jnp.where(is_first, before, moved)
                cv_v[r0 : r0 + PR, c] = mean(here, tp_v[r0 + 1 : r0 + PR + 1, c])
            before = moved
    for q in range(nq):
        c = slice(q * L, (q + 1) * L)
        r = slice(TOP + rows - 1, TOP + rows)
        cv_v[r, c] = jnp.where(me_r < nr - 1, cv_v[r, c], 0.0)

    load_p.wait()
    load_cnt.wait()
    row_e = lax.broadcasted_iota(jnp.int32, (H, L), 0)
    lo_count = jnp.where(me_r > 0, cnt_s[0, 0], 0)
    hi_count = jnp.where(me_r < nr - 1, cnt_s[0, 1], 0)

    for copy in tile_copies:
        copy.wait_recv()
    total = tile_s[8:16, :]
    for k in range(1, nc):
        total = total + tile_r[k, 8:16, :]
    total = total[0:1, :]
    coarse = jnp.zeros((8, L), F32)
    for k in range(nc):
        part = tile_s[0:8, :] if k == 0 else tile_r[k, 0:8, :]
        owner = lax.rem(me_c - k + nc, nc)
        value = jnp.sum(part * total, axis=1, keepdims=True)
        coarse = coarse + jnp.where(lane8 == owner * kmax + sub8, value, 0.0)
    coarse = jnp.sum(coarse, axis=0, keepdims=True)
    for q in range(nq):
        corr = jnp.sum(jnp.where(hot[q], coarse, 0.0), axis=1, keepdims=True)
        corr_v[0:npr, q * L : (q + 1) * L] = jnp.broadcast_to(corr, (npr, L))

    edge_c = []
    edge_r = []
    for n, w in enumerate(order):
        for copy in halos[n]:
            copy.wait_recv()
        for q in (2 * w, 2 * w + 1):
            c = slice(q * L, (q + 1) * L)
            low = jnp.where(row_e >= H - lo_count, halo_v[0, :, c], 0.0)
            high = jnp.where(row_e < hi_count, halo_v[1, :, c], 0.0)
            ext_v[0:H, c] = low.astype(BF16)
            ext_v[H + rows : 2 * H + rows, c] = high.astype(BF16)
            z = jnp.dot(pinv_v[q, H : H + rows, :], ext_v[:, c], preferred_element_type=F32)
            for p in range(npr):
                dp = z[p * PR : (p + 1) * PR, :] + corr_v[p : p + 1, c]
                dp_v[TOP + p * PR : TOP + (p + 1) * PR, c] = dp
                if p == 0:
                    drow_s[0, :, c] = dp[0:1, :]
                    dp_v[TOP - 1 : TOP, c] = dp[0:1, :]
                if p == npr - 1:
                    drow_s[1, :, c] = dp[PR - 1 : PR, :]
                    dp_v[TOP + rows : TOP + rows + 1, c] = dp[PR - 1 : PR, :]
        span = pl.ds(w * 2 * L, 2 * L)
        edge_r.append(send(drow_s.at[0, :, span], drow_r.at[1, :, span], 12 + 2 * n, (down, me_c)))
        edge_r.append(send(drow_s.at[1, :, span], drow_r.at[0, :, span], 13 + 2 * n, (up, me_c)))
        if w == pairs - 1:
            edge_c.append(send(dp_v.at[body, last], dcol_r.at[0], 20, (me_r, right)))
        if w == 0:
            edge_c.append(send(dp_v.at[body, first], dcol_r.at[1], 21, (me_r, left)))

    load_m.wait()
    load_a.wait()
    load_c.wait()

    def column(p, q):
        r0 = TOP + p * PR
        if q < 0:
            return dcol_r[0, p * PR : (p + 1) * PR, :]
        if q == nq:
            return dcol_r[1, p * PR : (p + 1) * PR, :]
        return dp_v[r0 : r0 + PR, q * L : (q + 1) * L]

    def finish(p, q):
        r0 = TOP + p * PR
        r = slice(p * PR, (p + 1) * PR)
        c = slice(q * L, (q + 1) * L)
        here = column(p, q)
        after = jnp.where(is_last, pltpu.roll(column(p, q + 1), L - 1, 1), pltpu.roll(here, L - 1, 1))
        prior = jnp.where(is_first, pltpu.roll(column(p, q - 1), 1, 1), pltpu.roll(here, 1, 1))
        flux = chr_v[r, c] * (here - after) + chl_v[r, c] * (here - prior)
        flux = flux + cv_v[r0 : r0 + PR, c] * (here - dp_v[r0 + 1 : r0 + PR + 1, c])
        flux = flux + cv_v[r0 - 1 : r0 + PR - 1, c] * (here - dp_v[r0 - 1 : r0 + PR - 1, c])
        r2 = [
            res_v[k, r, c]
            - (acc_v[k, r, c].astype(F32) * here + mob_v[k, r, c].astype(F32) * flux)
            for k in range(3)
        ]
        for k in range(3):
            u = cell_v[3 * k, r, c].astype(F32) * r2[0]
            u = u + cell_v[3 * k + 1, r, c].astype(F32) * r2[1]
            u = u + cell_v[3 * k + 2, r, c].astype(F32) * r2[2]
            if k == 0:
                u = u + here
            out_ref[k, r, c] = u

    for q in range(1, nq - 1):
        for p in range(npr):
            finish(p, q)
    for copy in edge_c:
        copy.wait_recv()
    for q in (0, nq - 1):
        for p in range(npr):
            finish(p, q)
    for copy in edge_r:
        copy.wait_recv()
    for q in range(nq):
        c = slice(q * L, (q + 1) * L)
        for e in range(2):
            r = slice(0, 8) if e == 0 else slice(rows - 8, rows)
            face = slice(TOP - 1, TOP) if e == 0 else slice(TOP + rows - 1, TOP + rows)
            mine = slice(TOP, TOP + 1) if e == 0 else slice(TOP + rows - 1, TOP + rows)
            extra = cv_v[face, c] * (dp_v[mine, c] - drow_r[e, :, c])
            extra = jnp.where(sub8 == (0 if e == 0 else 7), extra, 0.0)
            m = [mob_v[j, r, c].astype(F32) * extra for j in range(3)]
            for k in range(3):
                u = cell_v[3 * k, r, c].astype(F32) * m[0]
                u = u + cell_v[3 * k + 1, r, c].astype(F32) * m[1]
                u = u + cell_v[3 * k + 2, r, c].astype(F32) * m[2]
                out_ref[k, r, c] = out_ref[k, r, c] - u
    for copy in sent + tile_copies:
        copy.wait_send()


def place(in_ref, out_ref, sem):
    copy = pltpu.make_async_copy(in_ref, out_ref, sem.at[0])
    copy.start()
    copy.wait()


def shards(nr, nc, *args):
    residual, pinv = args[0], args[6]
    rows, cols = residual.shape[1:]
    groups = pinv.shape[1]
    e = rows + 2 * H
    hbm = pl.BlockSpec(memory_space=pl.ANY)
    vmem = pl.BlockSpec(memory_space=pltpu.VMEM)
    tall = rows + 2 * TOP
    scratch = [
        pltpu.VMEM((3, rows, cols), F32),
        pltpu.VMEM((3, rows, cols), F32),
        pltpu.VMEM((3, rows, cols), BF16),
        pltpu.VMEM((3, rows, cols), BF16),
        pltpu.VMEM((tall, cols), F32),
        pltpu.VMEM((9, rows, cols), BF16),
        pltpu.VMEM((groups, e, L), BF16),
        pltpu.VMEM(args[7].shape[2:], F32),
        pltpu.SMEM(args[8].shape, jnp.int32),
        pltpu.VMEM(args[9].shape, jnp.int32),
        pltpu.VMEM((rows, cols), F32),
        pltpu.VMEM((2, H, cols), F32),
        pltpu.VMEM((e, cols), BF16),
        pltpu.VMEM((2, 1, cols), F32),
        pltpu.VMEM((2, 1, cols), F32),
        pltpu.VMEM((2, rows, L), F32),
        pltpu.VMEM((2, 1, cols), F32),
        pltpu.VMEM((2, 1, cols), F32),
        pltpu.VMEM((2, rows, L), F32),
        pltpu.VMEM((tall, cols), F32),
        pltpu.VMEM((tall, cols), F32),
        pltpu.VMEM((rows, cols), F32),
        pltpu.VMEM((rows, cols), F32),
        pltpu.VMEM((8, cols), F32),
        pltpu.VMEM((16, L), F32),
        pltpu.VMEM((nc, 16, L), F32),
        pltpu.VMEM((8, cols), F32),
        pltpu.SemaphoreType.DMA((16,)),
        pltpu.SemaphoreType.DMA((22,)),
        pltpu.SemaphoreType.DMA((22,)),
        pltpu.SemaphoreType.DMA((nc,)),
        pltpu.SemaphoreType.DMA((nc,)),
    ]
    update = pl.pallas_call(
        functools.partial(kernel, nr, nc),
        out_shape=pltpu.VMEM((3, rows, cols), F32),
        in_specs=[hbm] * 10,
        out_specs=vmem,
        scratch_shapes=scratch,
        compiler_params=pltpu.CompilerParams(
            collective_id=0, has_side_effects=True, vmem_limit_bytes=60 * 1024 * 1024
        ),
    )(*args)
    return pl.pallas_call(
        place,
        out_shape=jax.ShapeDtypeStruct((3, rows, cols), F32),
        in_specs=[pl.BlockSpec(memory_space=pltpu.VMEM)],
        out_specs=pl.BlockSpec(memory_space=pl.ANY),
        scratch_shapes=[pltpu.SemaphoreType.DMA((1,))],
        compiler_params=pltpu.CompilerParams(vmem_limit_bytes=1024 * 1024),
    )(update)


def solution(mesh):
    in_specs = (
        P(None, "rows", "cols"),
        P(None, "rows", "cols"),
        P(None, "rows", "cols"),
        P(None, "rows", "cols"),
        P("rows", "cols"),
        P(None, "rows", "cols"),
        P("rows", "cols", None, None),
        P("rows", "cols", None, None),
        P("rows", None),
        P("rows", "cols"),
    )
    out_specs = P(None, "rows", "cols")
    body = functools.partial(shards, mesh.shape["rows"], mesh.shape["cols"])
    return jax.shard_map(body, mesh=mesh, in_specs=in_specs, out_specs=out_specs, check_vma=False)
```

```python
import functools
import math

import jax
import jax.numpy as jnp
from jax import lax
from jax.experimental import pallas as pl
from jax.experimental.pallas import tpu as pltpu
from jax.sharding import PartitionSpec as P

H = 32
PR = 16
PC = 128
L = 128
TOP = 8
MESH = pl.DeviceIdType.MESH
F32 = jnp.float32
BF16 = jnp.bfloat16


def kernel(
    nr, nc,
    res_h, wts_h, acc_h, mob_h, trans_h, cell_h, pinv_h, ci_h, cnt_h, slot_h,
    out_ref,
    res_v, wts_v, acc_v, mob_v, tp_v, cell_v, pinv_v, ci_v, cnt_s, slot_v,
    rp_v, halo_v, ext_v, trow_s, trow_r, tcol_r, drow_s, drow_r, dcol_r, dp_v, cv_v, chr_v, chl_v,
    ps_v, tile_s, tile_r, corr_v,
    load_sem, send_sem, recv_sem, tile_send, tile_recv,
):
    rows = trans_h.shape[0]
    cols = trans_h.shape[1]
    nq = cols // L
    npr = rows // PR
    kmax = ci_h.shape[-1]
    pairs = nq // 2
    order = [pairs - 1] + list(range(pairs - 1))
    me_r = lax.axis_index("rows")
    me_c = lax.axis_index("cols")
    up = lax.rem(me_r + 1, nr)
    down = lax.rem(me_r + nr - 1, nr)
    right = lax.rem(me_c + 1, nc)
    left = lax.rem(me_c + nc - 1, nc)

    def load(src, dst, i):
        copy = pltpu.make_async_copy(src, dst, load_sem.at[i])
        copy.start()
        return copy

    rw = []
    for n, w in enumerate(order):
        span = pl.ds(w * 2 * L, 2 * L)
        rw.append((
            load(res_h.at[:, :, span], res_v.at[:, :, span], 2 * n),
            load(wts_h.at[:, :, span], wts_v.at[:, :, span], 2 * n + 1),
        ))
        if n == 0:
            load_t = load(trans_h, tp_v.at[pl.ds(TOP, rows), :], 8)
            load_ci = load(ci_h.at[0, 0], ci_v, 9)
            load_slot = load(slot_h, slot_v, 10)
            load_cnt = load(cnt_h, cnt_s, 11)
    barrier = pltpu.get_barrier_semaphore()
    has_down = me_r > 0
    has_up = me_r < nr - 1
    has_left = me_c > 0
    has_right = me_c < nc - 1
    for target, there in ((up, has_up), (down, has_down)):
        @pl.when(there)
        def _():
            pl.semaphore_signal(barrier, inc=1, device_id=(target, me_c), device_id_type=MESH)
    for k in range(1, nc):
        pl.semaphore_signal(
            barrier, inc=1, device_id=(me_r, lax.rem(me_c + k, nc)), device_id_type=MESH
        )

    sent = []

    ways = {
        "down": ((down, me_c), has_down, has_up),
        "up": ((up, me_c), has_up, has_down),
        "left": ((me_r, left), has_left, has_right),
        "right": ((me_r, right), has_right, has_left),
    }

    def send(src, dst, i, way):
        device, goes, comes = ways[way]
        copy = pltpu.make_async_remote_copy(
            src_ref=src, dst_ref=dst, send_sem=send_sem.at[i], recv_sem=recv_sem.at[i],
            device_id=device, device_id_type=MESH,
        )
        pl.when(goes)(copy.start)
        sent.append((copy, goes))
        return copy, comes

    def arrive(copies):
        for copy, comes in copies:
            pl.when(comes)(copy.wait_recv)

    body = pl.ds(TOP, rows)
    first = pl.ds(0, L)
    last = pl.ds(cols - L, L)
    halos = []
    for n, w in enumerate(order):
        rw[n][0].wait()
        rw[n][1].wait()
        for q in (2 * w, 2 * w + 1):
            c = slice(q * L, (q + 1) * L)
            for p in range(npr):
                r = slice(p * PR, (p + 1) * PR)
                rp = res_v[0, r, c] * wts_v[0, r, c]
                rp = rp + res_v[1, r, c] * wts_v[1, r, c]
                rp = rp + res_v[2, r, c] * wts_v[2, r, c]
                rp_v[r, c] = rp
                ext_v[H + p * PR : H + (p + 1) * PR, c] = rp.astype(BF16)
                ps_v[p : p + 1, c] = jnp.sum(rp, axis=0, keepdims=True)
        if n == 0:
            pl.semaphore_wait(barrier, nc - 1 + has_down.astype(jnp.int32) + has_up.astype(jnp.int32))
        span = pl.ds(w * 2 * L, 2 * L)
        halos.append((
            send(rp_v.at[pl.ds(0, H), span], halo_v.at[1, :, span], 2 * n, "down"),
            send(rp_v.at[pl.ds(H, H), span], halo_v.at[0, :, span], 2 * n + 1, "up"),
        ))
        if n == 0:
            load_t.wait()
            trow_s[0] = tp_v[TOP : TOP + 1, :]
            trow_s[1] = tp_v[TOP + rows - 1 : TOP + rows, :]
            edge_t = [
                send(tp_v.at[body, first], tcol_r.at[1], 8, "left"),
                send(tp_v.at[body, last], tcol_r.at[0], 9, "right"),
                send(trow_s.at[0], trow_r.at[1], 10, "down"),
                send(trow_s.at[1], trow_r.at[0], 11, "up"),
            ]

    load_p = load(pinv_h.at[0], pinv_v, 12)
    load_m = load(mob_h, mob_v, 13)
    load_a = load(acc_h, acc_v, 14)
    load_c = load(cell_h, cell_v, 15)

    load_ci.wait()
    load_slot.wait()
    lane8 = lax.broadcasted_iota(jnp.int32, (8, L), 1)
    sub8 = lax.broadcasted_iota(jnp.int32, (8, L), 0)
    block = jnp.zeros((kmax, L), F32)
    own = ci_v[...]
    for j in range(kmax):
        block = block + jnp.where(lane8 == me_c * kmax + j, own[:, j : j + 1], 0.0)
    tile_s[0:8, :] = block
    tile_s[8:16, :] = jnp.zeros((8, L), F32)
    lane4 = lax.broadcasted_iota(jnp.int32, (npr, L), 1)
    slots = slot_v[...]
    tiles = jnp.zeros((npr, L), F32)
    hot = []
    for q in range(nq):
        sums = jnp.sum(ps_v[0:npr, q * L : (q + 1) * L], axis=1, keepdims=True)
        hit = lane4 == slots[:, q : q + 1]
        hot.append(hit)
        tiles = tiles + jnp.where(hit, sums, 0.0)
    tiles = jnp.sum(tiles, axis=0, keepdims=True) * (1.0 / math.sqrt(PR * PC))
    tile_s[8:9, :] = tiles
    tile_copies = []
    for k in range(1, nc):
        copy = pltpu.make_async_remote_copy(
            src_ref=tile_s, dst_ref=tile_r.at[k],
            send_sem=tile_send.at[k], recv_sem=tile_recv.at[k],
            device_id=(me_r, lax.rem(me_c + k, nc)), device_id_type=MESH,
        )
        copy.start()
        tile_copies.append(copy)

    for i, row, col in ((0, has_down, has_left), (1, has_up, has_right)):
        @pl.when(jnp.logical_not(row))
        def _():
            drow_r[i] = jnp.zeros(drow_r.shape[1:], F32)

        @pl.when(jnp.logical_not(col))
        def _():
            dcol_r[i] = jnp.zeros(dcol_r.shape[1:], F32)

    arrive(edge_t)
    tp_v[TOP - 1 : TOP, :] = trow_r[0]
    tp_v[TOP + rows : TOP + rows + 1, :] = trow_r[1]

    lane16 = lax.broadcasted_iota(jnp.int32, (PR, L), 1)
    is_last = lane16 == L - 1
    is_first = lane16 == 0

    def mean(a, b):
        return 2.0 * a * b / (a + b)

    for q in range(nq):
        c = slice(q * L, (q + 1) * L)
        low = mean(tp_v[TOP - 1 : TOP, c], tp_v[TOP : TOP + 1, c])
        cv_v[TOP - 1 : TOP, c] = jnp.where(me_r > 0, low, 0.0)
    for p in range(npr):
        r0 = TOP + p * PR
        r = slice(p * PR, (p + 1) * PR)
        blocks = [tcol_r[0, r, :]]
        blocks += [tp_v[r0 : r0 + PR, q * L : (q + 1) * L] for q in range(nq)]
        blocks += [tcol_r[1, r, :]]
        turned = [pltpu.roll(b, L - 1, 1) for b in blocks[1:]]
        before = None
        for q in range(nq + 1):
            here = blocks[q]
            if q == 0:
                near = turned[0]
            else:
                near = jnp.where(is_last, turned[q], turned[q - 1])
            face = mean(here, near)
            if q == 0:
                face = jnp.where(me_c > 0, face, 0.0)
            if q == nq:
                face = jnp.where(is_last & (me_c == nc - 1), 0.0, face)
            moved = pltpu.roll(face, 1, 1)
            if q > 0:
                c = slice((q - 1) * L, q * L)
                chr_v[r, c] = face
                chl_v[r, c] = jnp.where(is_first, before, moved)
                cv_v[r0 : r0 + PR, c] = mean(here, tp_v[r0 + 1 : r0 + PR + 1, c])
            before = moved
    for q in range(nq):
        c = slice(q * L, (q + 1) * L)
        r = slice(TOP + rows - 1, TOP + rows)
        cv_v[r, c] = jnp.where(me_r < nr - 1, cv_v[r, c], 0.0)

    load_p.wait()
    load_cnt.wait()
    row_e = lax.broadcasted_iota(jnp.int32, (H, L), 0)
    lo_count = jnp.where(me_r > 0, cnt_s[0, 0], 0)
    hi_count = jnp.where(me_r < nr - 1, cnt_s[0, 1], 0)

    for copy in tile_copies:
        copy.wait_recv()
    total = tile_s[8:16, :]
    for k in range(1, nc):
        total = total + tile_r[k, 8:16, :]
    total = total[0:1, :]
    coarse = jnp.zeros((8, L), F32)
    for k in range(nc):
        part = tile_s[0:8, :] if k == 0 else tile_r[k, 0:8, :]
        owner = lax.rem(me_c - k + nc, nc)
        value = jnp.sum(part * total, axis=1, keepdims=True)
        coarse = coarse + jnp.where(lane8 == owner * kmax + sub8, value, 0.0)
    coarse = jnp.sum(coarse, axis=0, keepdims=True)
    for q in range(nq):
        corr = jnp.sum(jnp.where(hot[q], coarse, 0.0), axis=1, keepdims=True)
        corr_v[0:npr, q * L : (q + 1) * L] = jnp.broadcast_to(corr, (npr, L))

    edge_c = []
    edge_r = []
    for n, w in enumerate(order):
        arrive(halos[n])
        for q in (2 * w, 2 * w + 1):
            c = slice(q * L, (q + 1) * L)
            low = jnp.where(row_e >= H - lo_count, halo_v[0, :, c], 0.0)
            high = jnp.where(row_e < hi_count, halo_v[1, :, c], 0.0)
            ext_v[0:H, c] = low.astype(BF16)
            ext_v[H + rows : 2 * H + rows, c] = high.astype(BF16)
            z = jnp.dot(pinv_v[q, H : H + rows, :], ext_v[:, c], preferred_element_type=F32)
            for p in range(npr):
                dp = z[p * PR : (p + 1) * PR, :] + corr_v[p : p + 1, c]
                dp_v[TOP + p * PR : TOP + (p + 1) * PR, c] = dp
                if p == 0:
                    drow_s[0, :, c] = dp[0:1, :]
                    dp_v[TOP - 1 : TOP, c] = dp[0:1, :]
                if p == npr - 1:
                    drow_s[1, :, c] = dp[PR - 1 : PR, :]
                    dp_v[TOP + rows : TOP + rows + 1, c] = dp[PR - 1 : PR, :]
        span = pl.ds(w * 2 * L, 2 * L)
        edge_r.append(send(drow_s.at[0, :, span], drow_r.at[1, :, span], 12 + 2 * n, "down"))
        edge_r.append(send(drow_s.at[1, :, span], drow_r.at[0, :, span], 13 + 2 * n, "up"))
        if w == pairs - 1:
            edge_c.append(send(dp_v.at[body, last], dcol_r.at[0], 20, "right"))
        if w == 0:
            edge_c.append(send(dp_v.at[body, first], dcol_r.at[1], 21, "left"))

    load_m.wait()
    load_a.wait()
    load_c.wait()

    def column(p, q):
        r0 = TOP + p * PR
        if q < 0:
            return dcol_r[0, p * PR : (p + 1) * PR, :]
        if q == nq:
            return dcol_r[1, p * PR : (p + 1) * PR, :]
        return dp_v[r0 : r0 + PR, q * L : (q + 1) * L]

    def finish(p, q):
        r0 = TOP + p * PR
        r = slice(p * PR, (p + 1) * PR)
        c = slice(q * L, (q + 1) * L)
        here = column(p, q)
        after = jnp.where(is_last, pltpu.roll(column(p, q + 1), L - 1, 1), pltpu.roll(here, L - 1, 1))
        prior = jnp.where(is_first, pltpu.roll(column(p, q - 1), 1, 1), pltpu.roll(here, 1, 1))
        flux = chr_v[r, c] * (here - after) + chl_v[r, c] * (here - prior)
        flux = flux + cv_v[r0 : r0 + PR, c] * (here - dp_v[r0 + 1 : r0 + PR + 1, c])
        flux = flux + cv_v[r0 - 1 : r0 + PR - 1, c] * (here - dp_v[r0 - 1 : r0 + PR - 1, c])
        r2 = [
            res_v[k, r, c]
            - (acc_v[k, r, c].astype(F32) * here + mob_v[k, r, c].astype(F32) * flux)
            for k in range(3)
        ]
        for k in range(3):
            u = cell_v[3 * k, r, c].astype(F32) * r2[0]
            u = u + cell_v[3 * k + 1, r, c].astype(F32) * r2[1]
            u = u + cell_v[3 * k + 2, r, c].astype(F32) * r2[2]
            if k == 0:
                u = u + here
            out_ref[k, r, c] = u

    for q in range(1, nq - 1):
        for p in range(npr):
            finish(p, q)
    arrive(edge_c)
    for q in (0, nq - 1):
        for p in range(npr):
            finish(p, q)
    arrive(edge_r)
    for q in range(nq):
        c = slice(q * L, (q + 1) * L)
        for e in range(2):
            r = slice(0, 8) if e == 0 else slice(rows - 8, rows)
            face = slice(TOP - 1, TOP) if e == 0 else slice(TOP + rows - 1, TOP + rows)
            mine = slice(TOP, TOP + 1) if e == 0 else slice(TOP + rows - 1, TOP + rows)
            extra = cv_v[face, c] * (dp_v[mine, c] - drow_r[e, :, c])
            extra = jnp.where(sub8 == (0 if e == 0 else 7), extra, 0.0)
            m = [mob_v[j, r, c].astype(F32) * extra for j in range(3)]
            for k in range(3):
                u = cell_v[3 * k, r, c].astype(F32) * m[0]
                u = u + cell_v[3 * k + 1, r, c].astype(F32) * m[1]
                u = u + cell_v[3 * k + 2, r, c].astype(F32) * m[2]
                out_ref[k, r, c] = out_ref[k, r, c] - u
    for copy, goes in sent:
        pl.when(goes)(copy.wait_send)
    for copy in tile_copies:
        copy.wait_send()


def place(in_ref, out_ref, sem):
    copy = pltpu.make_async_copy(in_ref, out_ref, sem.at[0])
    copy.start()
    copy.wait()


def shards(nr, nc, *args):
    residual, pinv = args[0], args[6]
    rows, cols = residual.shape[1:]
    groups = pinv.shape[1]
    e = rows + 2 * H
    hbm = pl.BlockSpec(memory_space=pl.ANY)
    vmem = pl.BlockSpec(memory_space=pltpu.VMEM)
    tall = rows + 2 * TOP
    scratch = [
        pltpu.VMEM((3, rows, cols), F32),
        pltpu.VMEM((3, rows, cols), F32),
        pltpu.VMEM((3, rows, cols), BF16),
        pltpu.VMEM((3, rows, cols), BF16),
        pltpu.VMEM((tall, cols), F32),
        pltpu.VMEM((9, rows, cols), BF16),
        pltpu.VMEM((groups, e, L), BF16),
        pltpu.VMEM(args[7].shape[2:], F32),
        pltpu.SMEM(args[8].shape, jnp.int32),
        pltpu.VMEM(args[9].shape, jnp.int32),
        pltpu.VMEM((rows, cols), F32),
        pltpu.VMEM((2, H, cols), F32),
        pltpu.VMEM((e, cols), BF16),
        pltpu.VMEM((2, 1, cols), F32),
        pltpu.VMEM((2, 1, cols), F32),
        pltpu.VMEM((2, rows, L), F32),
        pltpu.VMEM((2, 1, cols), F32),
        pltpu.VMEM((2, 1, cols), F32),
        pltpu.VMEM((2, rows, L), F32),
        pltpu.VMEM((tall, cols), F32),
        pltpu.VMEM((tall, cols), F32),
        pltpu.VMEM((rows, cols), F32),
        pltpu.VMEM((rows, cols), F32),
        pltpu.VMEM((8, cols), F32),
        pltpu.VMEM((16, L), F32),
        pltpu.VMEM((nc, 16, L), F32),
        pltpu.VMEM((8, cols), F32),
        pltpu.SemaphoreType.DMA((16,)),
        pltpu.SemaphoreType.DMA((22,)),
        pltpu.SemaphoreType.DMA((22,)),
        pltpu.SemaphoreType.DMA((nc,)),
        pltpu.SemaphoreType.DMA((nc,)),
    ]
    update = pl.pallas_call(
        functools.partial(kernel, nr, nc),
        out_shape=pltpu.VMEM((3, rows, cols), F32),
        in_specs=[hbm] * 10,
        out_specs=vmem,
        scratch_shapes=scratch,
        compiler_params=pltpu.CompilerParams(
            collective_id=0, has_side_effects=True, vmem_limit_bytes=60 * 1024 * 1024
        ),
    )(*args)
    return pl.pallas_call(
        place,
        out_shape=jax.ShapeDtypeStruct((3, rows, cols), F32),
        in_specs=[pl.BlockSpec(memory_space=pltpu.VMEM)],
        out_specs=pl.BlockSpec(memory_space=pl.ANY),
        scratch_shapes=[pltpu.SemaphoreType.DMA((1,))],
        compiler_params=pltpu.CompilerParams(vmem_limit_bytes=1024 * 1024),
    )(update)


def solution(mesh):
    in_specs = (
        P(None, "rows", "cols"),
        P(None, "rows", "cols"),
        P(None, "rows", "cols"),
        P(None, "rows", "cols"),
        P("rows", "cols"),
        P(None, "rows", "cols"),
        P("rows", "cols", None, None),
        P("rows", "cols", None, None),
        P("rows", None),
        P("rows", "cols"),
    )
    out_specs = P(None, "rows", "cols")
    body = functools.partial(shards, mesh.shape["rows"], mesh.shape["cols"])
    return jax.shard_map(body, mesh=mesh, in_specs=in_specs, out_specs=out_specs, check_vma=False)
```

```python
import functools
import math

import jax
import jax.numpy as jnp
from jax import lax
from jax.experimental import pallas as pl
from jax.experimental.pallas import tpu as pltpu
from jax.sharding import PartitionSpec as P

H = 32
PR = 16
PC = 128
L = 128
TOP = 8
MESH = pl.DeviceIdType.MESH
F32 = jnp.float32
BF16 = jnp.bfloat16


def kernel(
    nr, nc,
    res_h, wts_h, acc_h, mob_h, trans_h, cell_h, pinv_h, ci_h, cnt_h, slot_h,
    out_ref,
    res_v, wts_v, acc_v, mob_v, tp_v, cell_v, pinv_v, ci_v, cnt_s, slot_v,
    rp_v, halo_v, ext_v, trow_s, trow_r, tcol_r, drow_s, drow_r, dcol_r, dp_v, cv_v, chr_v, chl_v,
    ps_v, tile_s, tile_r, corr_v, w_s, w_r, lo_v, add_v,
    load_sem, send_sem, recv_sem, tile_send, tile_recv,
):
    rows = trans_h.shape[0]
    cols = trans_h.shape[1]
    nq = cols // L
    npr = rows // PR
    kmax = ci_h.shape[-1]
    pairs = nq // 2
    order = [pairs - 1] + list(range(pairs - 1))
    me_r = lax.axis_index("rows")
    me_c = lax.axis_index("cols")
    up = lax.rem(me_r + 1, nr)
    down = lax.rem(me_r + nr - 1, nr)
    right = lax.rem(me_c + 1, nc)
    left = lax.rem(me_c + nc - 1, nc)

    def load(src, dst, i):
        copy = pltpu.make_async_copy(src, dst, load_sem.at[i])
        copy.start()
        return copy

    rw = []
    for n, w in enumerate(order):
        span = pl.ds(w * 2 * L, 2 * L)
        rw.append((
            load(res_h.at[:, :, span], res_v.at[:, :, span], 2 * n),
            load(wts_h.at[:, :, span], wts_v.at[:, :, span], 2 * n + 1),
        ))
        if n == 0:
            load_t = load(trans_h, tp_v.at[pl.ds(TOP, rows), :], 8)
            load_ci = load(ci_h.at[0, 0], ci_v, 9)
            load_slot = load(slot_h, slot_v, 10)
            load_cnt = load(cnt_h, cnt_s, 11)
    load_p = load(pinv_h.at[0], pinv_v, 12)

    barrier = pltpu.get_barrier_semaphore()
    has_down = me_r > 0
    has_up = me_r < nr - 1
    has_left = me_c > 0
    has_right = me_c < nc - 1
    for target, there in ((up, has_up), (down, has_down)):
        @pl.when(there)
        def _():
            pl.semaphore_signal(barrier, inc=1, device_id=(target, me_c), device_id_type=MESH)
    for k in range(1, nc):
        pl.semaphore_signal(
            barrier, inc=1, device_id=(me_r, lax.rem(me_c + k, nc)), device_id_type=MESH
        )

    sent = []

    ways = {
        "down": ((down, me_c), has_down, has_up),
        "up": ((up, me_c), has_up, has_down),
        "left": ((me_r, left), has_left, has_right),
        "right": ((me_r, right), has_right, has_left),
    }

    def send(src, dst, i, way):
        device, goes, comes = ways[way]
        copy = pltpu.make_async_remote_copy(
            src_ref=src, dst_ref=dst, send_sem=send_sem.at[i], recv_sem=recv_sem.at[i],
            device_id=device, device_id_type=MESH,
        )
        pl.when(goes)(copy.start)
        sent.append((copy, goes))
        return copy, comes

    def arrive(copies):
        for copy, comes in copies:
            pl.when(comes)(copy.wait_recv)

    body = pl.ds(TOP, rows)
    first = pl.ds(0, L)
    last = pl.ds(cols - L, L)
    lane8 = lax.broadcasted_iota(jnp.int32, (8, L), 1)
    halos = []
    for n, w in enumerate(order):
        rw[n][0].wait()
        rw[n][1].wait()
        for q in (2 * w, 2 * w + 1):
            c = slice(q * L, (q + 1) * L)
            for p in range(npr):
                r = slice(p * PR, (p + 1) * PR)
                rp = res_v[0, r, c] * wts_v[0, r, c]
                rp = rp + res_v[1, r, c] * wts_v[1, r, c]
                rp = rp + res_v[2, r, c] * wts_v[2, r, c]
                rp_v[r, c] = rp
                ext_v[H + p * PR : H + (p + 1) * PR, c] = rp.astype(BF16)
                ps_v[p : p + 1, c] = jnp.sum(rp, axis=0, keepdims=True)
        if n == 0:
            pl.semaphore_wait(barrier, nc - 1 + has_down.astype(jnp.int32) + has_up.astype(jnp.int32))
        span = pl.ds(w * 2 * L, 2 * L)
        halos.append((
            send(rp_v.at[pl.ds(0, H), span], halo_v.at[1, :, span], 2 * n, "down"),
            send(rp_v.at[pl.ds(H, H), span], halo_v.at[0, :, span], 2 * n + 1, "up"),
        ))
        if n == 0:
            load_t.wait()
            trow_s[0] = tp_v[TOP : TOP + 1, :]
            trow_s[1] = tp_v[TOP + rows - 1 : TOP + rows, :]
            edge_t = [
                send(tp_v.at[body, first], tcol_r.at[1], 8, "left"),
                send(tp_v.at[body, last], tcol_r.at[0], 9, "right"),
                send(trow_s.at[0], trow_r.at[1], 10, "down"),
                send(trow_s.at[1], trow_r.at[0], 11, "up"),
            ]
        if n == 1:
            load_p.wait()
            load_cnt.wait()
            lo_count = jnp.where(me_r > 0, cnt_s[0, 0], 0)
            hi_count = jnp.where(me_r < nr - 1, cnt_s[0, 1], 0)
            for q in range(nq):
                w_s[0, q : q + 1, :] = pinv_v[q, H : H + PR, :].astype(F32)[0:1, :]
                w_s[1, q : q + 1, :] = pinv_v[q, H + rows - PR : H + rows, :].astype(F32)[PR - 1 : PR, :]
            below = (lane8 < H) & (lane8 >= H - lo_count)
            above = (lane8 >= H + rows) & (lane8 < H + rows + hi_count)
            w_s[0] = pltpu.roll(jnp.where(below, w_s[0], 0.0), H, 1)
            w_s[1] = pltpu.roll(jnp.where(above, w_s[1], 0.0), H, 1)
            edge_w = [
                send(w_s.at[1], w_r.at[0], 23, "up"),
                send(w_s.at[0], w_r.at[1], 22, "down"),
            ]

    load_m = load(mob_h, mob_v, 13)
    load_a = load(acc_h, acc_v, 14)
    load_c = load(cell_h, cell_v, 15)

    load_ci.wait()
    load_slot.wait()
    sub8 = lax.broadcasted_iota(jnp.int32, (8, L), 0)
    block = jnp.zeros((kmax, L), F32)
    own = ci_v[...]
    for j in range(kmax):
        block = block + jnp.where(lane8 == me_c * kmax + j, own[:, j : j + 1], 0.0)
    tile_s[0:8, :] = block
    tile_s[8:16, :] = jnp.zeros((8, L), F32)
    lane4 = lax.broadcasted_iota(jnp.int32, (npr, L), 1)
    slots = slot_v[...]
    tiles = jnp.zeros((npr, L), F32)
    hot = []
    for q in range(nq):
        sums = jnp.sum(ps_v[0:npr, q * L : (q + 1) * L], axis=1, keepdims=True)
        hit = lane4 == slots[:, q : q + 1]
        hot.append(hit)
        tiles = tiles + jnp.where(hit, sums, 0.0)
    tiles = jnp.sum(tiles, axis=0, keepdims=True) * (1.0 / math.sqrt(PR * PC))
    tile_s[8:9, :] = tiles
    tile_copies = []
    for k in range(1, nc):
        copy = pltpu.make_async_remote_copy(
            src_ref=tile_s, dst_ref=tile_r.at[k],
            send_sem=tile_send.at[k], recv_sem=tile_recv.at[k],
            device_id=(me_r, lax.rem(me_c + k, nc)), device_id_type=MESH,
        )
        copy.start()
        tile_copies.append(copy)

    for i, row, col in ((0, has_down, has_left), (1, has_up, has_right)):
        @pl.when(jnp.logical_not(row))
        def _():
            drow_r[i] = jnp.zeros(drow_r.shape[1:], F32)
            w_r[i] = jnp.zeros(w_r.shape[1:], F32)

        @pl.when(jnp.logical_not(col))
        def _():
            dcol_r[i] = jnp.zeros(dcol_r.shape[1:], F32)

    arrive(edge_t)
    tp_v[TOP - 1 : TOP, :] = trow_r[0]
    tp_v[TOP + rows : TOP + rows + 1, :] = trow_r[1]

    lane16 = lax.broadcasted_iota(jnp.int32, (PR, L), 1)
    is_last = lane16 == L - 1
    is_first = lane16 == 0

    def mean(a, b):
        return 2.0 * a * b / (a + b)

    for q in range(nq):
        c = slice(q * L, (q + 1) * L)
        low = mean(tp_v[TOP - 1 : TOP, c], tp_v[TOP : TOP + 1, c])
        cv_v[TOP - 1 : TOP, c] = jnp.where(me_r > 0, low, 0.0)
    for p in range(npr):
        r0 = TOP + p * PR
        r = slice(p * PR, (p + 1) * PR)
        blocks = [tcol_r[0, r, :]]
        blocks += [tp_v[r0 : r0 + PR, q * L : (q + 1) * L] for q in range(nq)]
        blocks += [tcol_r[1, r, :]]
        turned = [pltpu.roll(b, L - 1, 1) for b in blocks[1:]]
        before = None
        for q in range(nq + 1):
            here = blocks[q]
            if q == 0:
                near = turned[0]
            else:
                near = jnp.where(is_last, turned[q], turned[q - 1])
            face = mean(here, near)
            if q == 0:
                face = jnp.where(me_c > 0, face, 0.0)
            if q == nq:
                face = jnp.where(is_last & (me_c == nc - 1), 0.0, face)
            moved = pltpu.roll(face, 1, 1)
            if q > 0:
                c = slice((q - 1) * L, q * L)
                chr_v[r, c] = face
                chl_v[r, c] = jnp.where(is_first, before, moved)
                cv_v[r0 : r0 + PR, c] = mean(here, tp_v[r0 + 1 : r0 + PR + 1, c])
            before = moved
    for q in range(nq):
        c = slice(q * L, (q + 1) * L)
        r = slice(TOP + rows - 1, TOP + rows)
        cv_v[r, c] = jnp.where(me_r < nr - 1, cv_v[r, c], 0.0)

    row_e = lax.broadcasted_iota(jnp.int32, (H, L), 0)

    for copy in tile_copies:
        copy.wait_recv()
    total = tile_s[8:16, :]
    for k in range(1, nc):
        total = total + tile_r[k, 8:16, :]
    total = total[0:1, :]
    coarse = jnp.zeros((8, L), F32)
    for k in range(nc):
        part = tile_s[0:8, :] if k == 0 else tile_r[k, 0:8, :]
        owner = lax.rem(me_c - k + nc, nc)
        value = jnp.sum(part * total, axis=1, keepdims=True)
        coarse = coarse + jnp.where(lane8 == owner * kmax + sub8, value, 0.0)
    coarse = jnp.sum(coarse, axis=0, keepdims=True)
    for q in range(nq):
        corr = jnp.sum(jnp.where(hot[q], coarse, 0.0), axis=1, keepdims=True)
        corr_v[0:npr, q * L : (q + 1) * L] = jnp.broadcast_to(corr, (npr, L))

    edge_c = []
    edge_r = []

    def own_part(side):
        arrive(edge_w[side : side + 1])
        lhs = w_r[side].astype(BF16)[:, 0:rows]
        for q in range(nq):
            c = slice(q * L, (q + 1) * L)
            part = jnp.dot(lhs, ext_v[H : H + rows, c], preferred_element_type=F32)
            add_v[side, :, c] = part[q : q + 1, :]

    for n, w in enumerate(order):
        if n == pairs - 1:
            own_part(0)
        arrive(halos[n][1:2])
        for q in (2 * w, 2 * w + 1):
            c = slice(q * L, (q + 1) * L)
            low = jnp.where(row_e >= H - lo_count, halo_v[0, :, c], 0.0)
            ext_v[0:H, c] = low.astype(BF16)
            top = jnp.dot(
                pinv_v[q, H + rows - PR : H + rows, :][:, 0 : H + rows], ext_v[0 : H + rows, c],
                preferred_element_type=F32,
            )
            drow_s[1, :, c] = top[PR - 1 : PR, :] + corr_v[npr - 1 : npr, c]
            low = jnp.dot(
                pinv_v[q, H : H + PR, :][:, 0:H], ext_v[0:H, c], preferred_element_type=F32
            )
            lo_v[0:1, c] = low[0:1, :]
        span = pl.ds(w * 2 * L, 2 * L)
        edge_r.append(send(drow_s.at[1, :, span], drow_r.at[0, :, span], 13 + 2 * n, "up"))
    for n, w in enumerate(order):
        if n == pairs - 1:
            own_part(1)
        arrive(halos[n][0:1])
        for q in (2 * w, 2 * w + 1):
            c = slice(q * L, (q + 1) * L)
            high = jnp.where(row_e < hi_count, halo_v[1, :, c], 0.0)
            ext_v[H + rows : 2 * H + rows, c] = high.astype(BF16)
            z = jnp.dot(pinv_v[q, H : H + rows, :], ext_v[:, c], preferred_element_type=F32)
            for p in range(npr):
                dp = z[p * PR : (p + 1) * PR, :] + corr_v[p : p + 1, c]
                dp_v[TOP + p * PR : TOP + (p + 1) * PR, c] = dp
                if p == 0:
                    drow_s[0, :, c] = dp[0:1, :] - lo_v[0:1, c]
                    dp_v[TOP - 1 : TOP, c] = dp[0:1, :]
                if p == npr - 1:
                    dp_v[TOP + rows : TOP + rows + 1, c] = dp[PR - 1 : PR, :]
        span = pl.ds(w * 2 * L, 2 * L)
        edge_r.append(send(drow_s.at[0, :, span], drow_r.at[1, :, span], 12 + 2 * n, "down"))
        if w == pairs - 1:
            edge_c.append(send(dp_v.at[body, last], dcol_r.at[0], 20, "right"))
        if w == 0:
            edge_c.append(send(dp_v.at[body, first], dcol_r.at[1], 21, "left"))

    load_m.wait()
    load_a.wait()
    load_c.wait()

    def column(p, q):
        r0 = TOP + p * PR
        if q < 0:
            return dcol_r[0, p * PR : (p + 1) * PR, :]
        if q == nq:
            return dcol_r[1, p * PR : (p + 1) * PR, :]
        return dp_v[r0 : r0 + PR, q * L : (q + 1) * L]

    def finish(p, q):
        r0 = TOP + p * PR
        r = slice(p * PR, (p + 1) * PR)
        c = slice(q * L, (q + 1) * L)
        here = column(p, q)
        after = jnp.where(is_last, pltpu.roll(column(p, q + 1), L - 1, 1), pltpu.roll(here, L - 1, 1))
        prior = jnp.where(is_first, pltpu.roll(column(p, q - 1), 1, 1), pltpu.roll(here, 1, 1))
        flux = chr_v[r, c] * (here - after) + chl_v[r, c] * (here - prior)
        flux = flux + cv_v[r0 : r0 + PR, c] * (here - dp_v[r0 + 1 : r0 + PR + 1, c])
        flux = flux + cv_v[r0 - 1 : r0 + PR - 1, c] * (here - dp_v[r0 - 1 : r0 + PR - 1, c])
        r2 = [
            res_v[k, r, c]
            - (acc_v[k, r, c].astype(F32) * here + mob_v[k, r, c].astype(F32) * flux)
            for k in range(3)
        ]
        for k in range(3):
            u = cell_v[3 * k, r, c].astype(F32) * r2[0]
            u = u + cell_v[3 * k + 1, r, c].astype(F32) * r2[1]
            u = u + cell_v[3 * k + 2, r, c].astype(F32) * r2[2]
            if k == 0:
                u = u + here
            out_ref[k, r, c] = u

    for q in range(1, nq - 1):
        for p in range(npr):
            finish(p, q)
    arrive(edge_c)
    for q in (0, nq - 1):
        for p in range(npr):
            finish(p, q)
    arrive(edge_r)
    for q in range(nq):
        c = slice(q * L, (q + 1) * L)
        for e in range(2):
            r = slice(0, 8) if e == 0 else slice(rows - 8, rows)
            face = slice(TOP - 1, TOP) if e == 0 else slice(TOP + rows - 1, TOP + rows)
            mine = slice(TOP, TOP + 1) if e == 0 else slice(TOP + rows - 1, TOP + rows)
            extra = cv_v[face, c] * (dp_v[mine, c] - (drow_r[e, :, c] + add_v[e, :, c]))
            extra = jnp.where(sub8 == (0 if e == 0 else 7), extra, 0.0)
            m = [mob_v[j, r, c].astype(F32) * extra for j in range(3)]
            for k in range(3):
                u = cell_v[3 * k, r, c].astype(F32) * m[0]
                u = u + cell_v[3 * k + 1, r, c].astype(F32) * m[1]
                u = u + cell_v[3 * k + 2, r, c].astype(F32) * m[2]
                out_ref[k, r, c] = out_ref[k, r, c] - u
    for copy, goes in sent:
        pl.when(goes)(copy.wait_send)
    for copy in tile_copies:
        copy.wait_send()


def place(in_ref, out_ref, sem):
    copy = pltpu.make_async_copy(in_ref, out_ref, sem.at[0])
    copy.start()
    copy.wait()


def shards(nr, nc, *args):
    residual, pinv = args[0], args[6]
    rows, cols = residual.shape[1:]
    groups = pinv.shape[1]
    e = rows + 2 * H
    hbm = pl.BlockSpec(memory_space=pl.ANY)
    vmem = pl.BlockSpec(memory_space=pltpu.VMEM)
    tall = rows + 2 * TOP
    scratch = [
        pltpu.VMEM((3, rows, cols), F32),
        pltpu.VMEM((3, rows, cols), F32),
        pltpu.VMEM((3, rows, cols), BF16),
        pltpu.VMEM((3, rows, cols), BF16),
        pltpu.VMEM((tall, cols), F32),
        pltpu.VMEM((9, rows, cols), BF16),
        pltpu.VMEM((groups, e, L), BF16),
        pltpu.VMEM(args[7].shape[2:], F32),
        pltpu.SMEM(args[8].shape, jnp.int32),
        pltpu.VMEM(args[9].shape, jnp.int32),
        pltpu.VMEM((rows, cols), F32),
        pltpu.VMEM((2, H, cols), F32),
        pltpu.VMEM((e, cols), BF16),
        pltpu.VMEM((2, 1, cols), F32),
        pltpu.VMEM((2, 1, cols), F32),
        pltpu.VMEM((2, rows, L), F32),
        pltpu.VMEM((2, 1, cols), F32),
        pltpu.VMEM((2, 1, cols), F32),
        pltpu.VMEM((2, rows, L), F32),
        pltpu.VMEM((tall, cols), F32),
        pltpu.VMEM((tall, cols), F32),
        pltpu.VMEM((rows, cols), F32),
        pltpu.VMEM((rows, cols), F32),
        pltpu.VMEM((8, cols), F32),
        pltpu.VMEM((16, L), F32),
        pltpu.VMEM((nc, 16, L), F32),
        pltpu.VMEM((8, cols), F32),
        pltpu.VMEM((2, 8, L), F32),
        pltpu.VMEM((2, 8, L), F32),
        pltpu.VMEM((8, cols), F32),
        pltpu.VMEM((2, 1, cols), F32),
        pltpu.SemaphoreType.DMA((16,)),
        pltpu.SemaphoreType.DMA((24,)),
        pltpu.SemaphoreType.DMA((24,)),
        pltpu.SemaphoreType.DMA((nc,)),
        pltpu.SemaphoreType.DMA((nc,)),
    ]
    update = pl.pallas_call(
        functools.partial(kernel, nr, nc),
        out_shape=pltpu.VMEM((3, rows, cols), F32),
        in_specs=[hbm] * 10,
        out_specs=vmem,
        scratch_shapes=scratch,
        compiler_params=pltpu.CompilerParams(
            collective_id=0, has_side_effects=True, vmem_limit_bytes=60 * 1024 * 1024
        ),
    )(*args)
    return pl.pallas_call(
        place,
        out_shape=jax.ShapeDtypeStruct((3, rows, cols), F32),
        in_specs=[pl.BlockSpec(memory_space=pltpu.VMEM)],
        out_specs=pl.BlockSpec(memory_space=pl.ANY),
        scratch_shapes=[pltpu.SemaphoreType.DMA((1,))],
        compiler_params=pltpu.CompilerParams(vmem_limit_bytes=1024 * 1024),
    )(update)


def solution(mesh):
    in_specs = (
        P(None, "rows", "cols"),
        P(None, "rows", "cols"),
        P(None, "rows", "cols"),
        P(None, "rows", "cols"),
        P("rows", "cols"),
        P(None, "rows", "cols"),
        P("rows", "cols", None, None),
        P("rows", "cols", None, None),
        P("rows", None),
        P("rows", "cols"),
    )
    out_specs = P(None, "rows", "cols")
    body = functools.partial(shards, mesh.shape["rows"], mesh.shape["cols"])
    return jax.shard_map(body, mesh=mesh, in_specs=in_specs, out_specs=out_specs, check_vma=False)
```

```python
import functools
import math

import jax
import jax.numpy as jnp
from jax import lax
from jax.experimental import pallas as pl
from jax.experimental.pallas import tpu as pltpu
from jax.sharding import PartitionSpec as P

H = 32
PR = 16
PC = 128
L = 128
TOP = 8
MESH = pl.DeviceIdType.MESH
F32 = jnp.float32
BF16 = jnp.bfloat16


def kernel(
    nr, nc,
    res_h, wts_h, acc_h, mob_h, trans_h, cell_h, pinv_h, ci_h, cnt_h, slot_h,
    out_ref,
    res_v, wts_v, acc_v, mob_v, tp_v, cell_v, pinv_v, ci_v, cnt_s, slot_v,
    rp_v, halo_v, ext_v, trow_s, trow_r, tcol_r, drow_s, drow_r, dcol_r, dp_v, cv_v, chr_v, chl_v,
    ps_v, tile_s, tile_r, corr_v,
    load_sem, send_sem, recv_sem, tile_send, tile_recv,
):
    rows = trans_h.shape[0]
    cols = trans_h.shape[1]
    nq = cols // L
    npr = rows // PR
    kmax = ci_h.shape[-1]
    pairs = nq // 2
    order = [pairs - 1] + list(range(pairs - 1))
    me_r = lax.axis_index("rows")
    me_c = lax.axis_index("cols")
    up = lax.rem(me_r + 1, nr)
    down = lax.rem(me_r + nr - 1, nr)
    right = lax.rem(me_c + 1, nc)
    left = lax.rem(me_c + nc - 1, nc)

    def load(src, dst, i):
        copy = pltpu.make_async_copy(src, dst, load_sem.at[i])
        copy.start()
        return copy

    rw = []
    for n, w in enumerate(order):
        span = pl.ds(w * 2 * L, 2 * L)
        rw.append((
            load(res_h.at[:, :, span], res_v.at[:, :, span], 2 * n),
            load(wts_h.at[:, :, span], wts_v.at[:, :, span], 2 * n + 1),
        ))
        if n == 0:
            load_t = load(trans_h, tp_v.at[pl.ds(TOP, rows), :], 8)
            load_ci = load(ci_h.at[0, 0], ci_v, 9)
            load_slot = load(slot_h, slot_v, 10)
            load_cnt = load(cnt_h, cnt_s, 11)
    barrier = pltpu.get_barrier_semaphore()
    has_down = me_r > 0
    has_up = me_r < nr - 1
    has_left = me_c > 0
    has_right = me_c < nc - 1
    for target, there in ((up, has_up), (down, has_down)):
        @pl.when(there)
        def _():
            pl.semaphore_signal(barrier, inc=1, device_id=(target, me_c), device_id_type=MESH)
    for k in range(1, nc):
        pl.semaphore_signal(
            barrier, inc=1, device_id=(me_r, lax.rem(me_c + k, nc)), device_id_type=MESH
        )

    sent = []

    ways = {
        "down": ((down, me_c), has_down, has_up),
        "up": ((up, me_c), has_up, has_down),
        "left": ((me_r, left), has_left, has_right),
        "right": ((me_r, right), has_right, has_left),
    }

    def send(src, dst, i, way):
        device, goes, comes = ways[way]
        copy = pltpu.make_async_remote_copy(
            src_ref=src, dst_ref=dst, send_sem=send_sem.at[i], recv_sem=recv_sem.at[i],
            device_id=device, device_id_type=MESH,
        )
        pl.when(goes)(copy.start)
        sent.append((copy, goes))
        return copy, comes

    def arrive(copies):
        for copy, comes in copies:
            pl.when(comes)(copy.wait_recv)

    body = pl.ds(TOP, rows)
    first = pl.ds(0, L)
    last = pl.ds(cols - L, L)
    halos = []
    for n, w in enumerate(order):
        rw[n][0].wait()
        rw[n][1].wait()
        for q in (2 * w, 2 * w + 1):
            c = slice(q * L, (q + 1) * L)
            for p in range(npr):
                r = slice(p * PR, (p + 1) * PR)
                rp = res_v[0, r, c] * wts_v[0, r, c]
                rp = rp + res_v[1, r, c] * wts_v[1, r, c]
                rp = rp + res_v[2, r, c] * wts_v[2, r, c]
                rp_v[r, c] = rp
                ext_v[H + p * PR : H + (p + 1) * PR, c] = rp.astype(BF16)
                ps_v[p : p + 1, c] = jnp.sum(rp, axis=0, keepdims=True)
        if n == 0:
            pl.semaphore_wait(barrier, nc - 1 + has_down.astype(jnp.int32) + has_up.astype(jnp.int32))
        span = pl.ds(w * 2 * L, 2 * L)
        halos.append((
            send(rp_v.at[pl.ds(0, H), span], halo_v.at[1, :, span], 2 * n, "down"),
            send(rp_v.at[pl.ds(H, H), span], halo_v.at[0, :, span], 2 * n + 1, "up"),
        ))
        if n == 0:
            load_t.wait()
            trow_s[0] = tp_v[TOP : TOP + 1, :]
            trow_s[1] = tp_v[TOP + rows - 1 : TOP + rows, :]
            edge_t = [
                send(tp_v.at[body, first], tcol_r.at[1], 8, "left"),
                send(tp_v.at[body, last], tcol_r.at[0], 9, "right"),
                send(trow_s.at[0], trow_r.at[1], 10, "down"),
                send(trow_s.at[1], trow_r.at[0], 11, "up"),
            ]

    load_p = load(pinv_h.at[0], pinv_v, 12)
    load_m = load(mob_h, mob_v, 13)
    load_a = load(acc_h, acc_v, 14)
    load_c = load(cell_h, cell_v, 15)

    load_ci.wait()
    load_slot.wait()
    lane8 = lax.broadcasted_iota(jnp.int32, (8, L), 1)
    sub8 = lax.broadcasted_iota(jnp.int32, (8, L), 0)
    block = jnp.zeros((kmax, L), F32)
    own = ci_v[...]
    for j in range(kmax):
        block = block + jnp.where(lane8 == me_c * kmax + j, own[:, j : j + 1], 0.0)
    tile_s[0:8, :] = block
    tile_s[8:16, :] = jnp.zeros((8, L), F32)
    lane4 = lax.broadcasted_iota(jnp.int32, (npr, L), 1)
    slots = slot_v[...]
    tiles = jnp.zeros((npr, L), F32)
    hot = []
    for q in range(nq):
        sums = jnp.sum(ps_v[0:npr, q * L : (q + 1) * L], axis=1, keepdims=True)
        hit = lane4 == slots[:, q : q + 1]
        hot.append(hit)
        tiles = tiles + jnp.where(hit, sums, 0.0)
    tiles = jnp.sum(tiles, axis=0, keepdims=True) * (1.0 / math.sqrt(PR * PC))
    tile_s[8:9, :] = tiles
    tile_copies = []
    for k in range(1, nc):
        copy = pltpu.make_async_remote_copy(
            src_ref=tile_s, dst_ref=tile_r.at[k],
            send_sem=tile_send.at[k], recv_sem=tile_recv.at[k],
            device_id=(me_r, lax.rem(me_c + k, nc)), device_id_type=MESH,
        )
        copy.start()
        tile_copies.append(copy)

    for i, row, col in ((0, has_down, has_left), (1, has_up, has_right)):
        @pl.when(jnp.logical_not(row))
        def _():
            drow_r[i] = jnp.zeros(drow_r.shape[1:], F32)

        @pl.when(jnp.logical_not(col))
        def _():
            dcol_r[i] = jnp.zeros(dcol_r.shape[1:], F32)

    arrive(edge_t)
    tp_v[TOP - 1 : TOP, :] = trow_r[0]
    tp_v[TOP + rows : TOP + rows + 1, :] = trow_r[1]

    lane16 = lax.broadcasted_iota(jnp.int32, (PR, L), 1)
    is_last = lane16 == L - 1
    is_first = lane16 == 0

    def mean(a, b):
        return 2.0 * a * b / (a + b)

    for q in range(nq):
        c = slice(q * L, (q + 1) * L)
        low = mean(tp_v[TOP - 1 : TOP, c], tp_v[TOP : TOP + 1, c])
        cv_v[TOP - 1 : TOP, c] = jnp.where(me_r > 0, low, 0.0)
    for p in range(npr):
        r0 = TOP + p * PR
        r = slice(p * PR, (p + 1) * PR)
        blocks = [tcol_r[0, r, :]]
        blocks += [tp_v[r0 : r0 + PR, q * L : (q + 1) * L] for q in range(nq)]
        blocks += [tcol_r[1, r, :]]
        turned = [pltpu.roll(b, L - 1, 1) for b in blocks[1:]]
        before = None
        for q in range(nq + 1):
            here = blocks[q]
            if q == 0:
                near = turned[0]
            else:
                near = jnp.where(is_last, turned[q], turned[q - 1])
            face = mean(here, near)
            if q == 0:
                face = jnp.where(me_c > 0, face, 0.0)
            if q == nq:
                face = jnp.where(is_last & (me_c == nc - 1), 0.0, face)
            moved = pltpu.roll(face, 1, 1)
            if q > 0:
                c = slice((q - 1) * L, q * L)
                chr_v[r, c] = face
                chl_v[r, c] = jnp.where(is_first, before, moved)
                cv_v[r0 : r0 + PR, c] = mean(here, tp_v[r0 + 1 : r0 + PR + 1, c])
            before = moved
    for q in range(nq):
        c = slice(q * L, (q + 1) * L)
        r = slice(TOP + rows - 1, TOP + rows)
        cv_v[r, c] = jnp.where(me_r < nr - 1, cv_v[r, c], 0.0)

    load_p.wait()
    load_cnt.wait()
    row_e = lax.broadcasted_iota(jnp.int32, (H, L), 0)
    lo_count = jnp.where(me_r > 0, cnt_s[0, 0], 0)
    hi_count = jnp.where(me_r < nr - 1, cnt_s[0, 1], 0)

    for copy in tile_copies:
        copy.wait_recv()
    total = tile_s[8:16, :]
    for k in range(1, nc):
        total = total + tile_r[k, 8:16, :]
    total = total[0:1, :]
    coarse = jnp.zeros((8, L), F32)
    for k in range(nc):
        part = tile_s[0:8, :] if k == 0 else tile_r[k, 0:8, :]
        owner = lax.rem(me_c - k + nc, nc)
        value = jnp.sum(part * total, axis=1, keepdims=True)
        coarse = coarse + jnp.where(lane8 == owner * kmax + sub8, value, 0.0)
    coarse = jnp.sum(coarse, axis=0, keepdims=True)
    for q in range(nq):
        corr = jnp.sum(jnp.where(hot[q], coarse, 0.0), axis=1, keepdims=True)
        corr_v[0:npr, q * L : (q + 1) * L] = jnp.broadcast_to(corr, (npr, L))

    def column(p, q):
        r0 = TOP + p * PR
        if q < 0:
            return dcol_r[0, p * PR : (p + 1) * PR, :]
        if q == nq:
            return dcol_r[1, p * PR : (p + 1) * PR, :]
        return dp_v[r0 : r0 + PR, q * L : (q + 1) * L]

    def finish(p, q):
        r0 = TOP + p * PR
        r = slice(p * PR, (p + 1) * PR)
        c = slice(q * L, (q + 1) * L)
        here = column(p, q)
        after = jnp.where(is_last, pltpu.roll(column(p, q + 1), L - 1, 1), pltpu.roll(here, L - 1, 1))
        prior = jnp.where(is_first, pltpu.roll(column(p, q - 1), 1, 1), pltpu.roll(here, 1, 1))
        flux = chr_v[r, c] * (here - after) + chl_v[r, c] * (here - prior)
        flux = flux + cv_v[r0 : r0 + PR, c] * (here - dp_v[r0 + 1 : r0 + PR + 1, c])
        flux = flux + cv_v[r0 - 1 : r0 + PR - 1, c] * (here - dp_v[r0 - 1 : r0 + PR - 1, c])
        r2 = [
            res_v[k, r, c]
            - (acc_v[k, r, c].astype(F32) * here + mob_v[k, r, c].astype(F32) * flux)
            for k in range(3)
        ]
        for k in range(3):
            u = cell_v[3 * k, r, c].astype(F32) * r2[0]
            u = u + cell_v[3 * k + 1, r, c].astype(F32) * r2[1]
            u = u + cell_v[3 * k + 2, r, c].astype(F32) * r2[2]
            if k == 0:
                u = u + here
            out_ref[k, r, c] = u

    edge_c = []
    edge_r = []
    for n, w in enumerate(order):
        arrive(halos[n])
        for q in (2 * w, 2 * w + 1):
            c = slice(q * L, (q + 1) * L)
            low = jnp.where(row_e >= H - lo_count, halo_v[0, :, c], 0.0)
            high = jnp.where(row_e < hi_count, halo_v[1, :, c], 0.0)
            ext_v[0:H, c] = low.astype(BF16)
            ext_v[H + rows : 2 * H + rows, c] = high.astype(BF16)
            z = jnp.dot(pinv_v[q, H : H + rows, :], ext_v[:, c], preferred_element_type=F32)
            for p in range(npr):
                dp = z[p * PR : (p + 1) * PR, :] + corr_v[p : p + 1, c]
                dp_v[TOP + p * PR : TOP + (p + 1) * PR, c] = dp
                if p == 0:
                    drow_s[0, :, c] = dp[0:1, :]
                    dp_v[TOP - 1 : TOP, c] = dp[0:1, :]
                if p == npr - 1:
                    drow_s[1, :, c] = dp[PR - 1 : PR, :]
                    dp_v[TOP + rows : TOP + rows + 1, c] = dp[PR - 1 : PR, :]
        span = pl.ds(w * 2 * L, 2 * L)
        edge_r.append(send(drow_s.at[0, :, span], drow_r.at[1, :, span], 12 + 2 * n, "down"))
        edge_r.append(send(drow_s.at[1, :, span], drow_r.at[0, :, span], 13 + 2 * n, "up"))
        if w == pairs - 1:
            edge_c.append(send(dp_v.at[body, last], dcol_r.at[0], 20, "right"))
        if w == 0:
            edge_c.append(send(dp_v.at[body, first], dcol_r.at[1], 21, "left"))
        if n == pairs - 2:
            load_m.wait()
            load_a.wait()
            load_c.wait()
            for q in range(1, nq - 5):
                for p in range(npr):
                    finish(p, q)

    for q in range(nq - 5, nq - 1):
        for p in range(npr):
            finish(p, q)
    arrive(edge_c)
    for q in (0, nq - 1):
        for p in range(npr):
            finish(p, q)
    arrive(edge_r)
    for q in range(nq):
        c = slice(q * L, (q + 1) * L)
        for e in range(2):
            r = slice(0, 8) if e == 0 else slice(rows - 8, rows)
            face = slice(TOP - 1, TOP) if e == 0 else slice(TOP + rows - 1, TOP + rows)
            mine = slice(TOP, TOP + 1) if e == 0 else slice(TOP + rows - 1, TOP + rows)
            extra = cv_v[face, c] * (dp_v[mine, c] - drow_r[e, :, c])
            extra = jnp.where(sub8 == (0 if e == 0 else 7), extra, 0.0)
            m = [mob_v[j, r, c].astype(F32) * extra for j in range(3)]
            for k in range(3):
                u = cell_v[3 * k, r, c].astype(F32) * m[0]
                u = u + cell_v[3 * k + 1, r, c].astype(F32) * m[1]
                u = u + cell_v[3 * k + 2, r, c].astype(F32) * m[2]
                out_ref[k, r, c] = out_ref[k, r, c] - u
    for copy, goes in sent:
        pl.when(goes)(copy.wait_send)
    for copy in tile_copies:
        copy.wait_send()


def place(in_ref, out_ref, sem):
    step = in_ref.shape[1] // 4
    copies = []
    for k in range(in_ref.shape[0]):
        for p in range(4):
            part = (k, pl.ds(p * step, step))
            copies.append(pltpu.make_async_copy(in_ref.at[part], out_ref.at[part], sem.at[4 * k + p]))
    for copy in copies:
        copy.start()
    for copy in copies:
        copy.wait()


def shards(nr, nc, *args):
    residual, pinv = args[0], args[6]
    rows, cols = residual.shape[1:]
    groups = pinv.shape[1]
    e = rows + 2 * H
    hbm = pl.BlockSpec(memory_space=pl.ANY)
    vmem = pl.BlockSpec(memory_space=pltpu.VMEM)
    tall = rows + 2 * TOP
    scratch = [
        pltpu.VMEM((3, rows, cols), F32),
        pltpu.VMEM((3, rows, cols), F32),
        pltpu.VMEM((3, rows, cols), BF16),
        pltpu.VMEM((3, rows, cols), BF16),
        pltpu.VMEM((tall, cols), F32),
        pltpu.VMEM((9, rows, cols), BF16),
        pltpu.VMEM((groups, e, L), BF16),
        pltpu.VMEM(args[7].shape[2:], F32),
        pltpu.SMEM(args[8].shape, jnp.int32),
        pltpu.VMEM(args[9].shape, jnp.int32),
        pltpu.VMEM((rows, cols), F32),
        pltpu.VMEM((2, H, cols), F32),
        pltpu.VMEM((e, cols), BF16),
        pltpu.VMEM((2, 1, cols), F32),
        pltpu.VMEM((2, 1, cols), F32),
        pltpu.VMEM((2, rows, L), F32),
        pltpu.VMEM((2, 1, cols), F32),
        pltpu.VMEM((2, 1, cols), F32),
        pltpu.VMEM((2, rows, L), F32),
        pltpu.VMEM((tall, cols), F32),
        pltpu.VMEM((tall, cols), F32),
        pltpu.VMEM((rows, cols), F32),
        pltpu.VMEM((rows, cols), F32),
        pltpu.VMEM((8, cols), F32),
        pltpu.VMEM((16, L), F32),
        pltpu.VMEM((nc, 16, L), F32),
        pltpu.VMEM((8, cols), F32),
        pltpu.SemaphoreType.DMA((16,)),
        pltpu.SemaphoreType.DMA((22,)),
        pltpu.SemaphoreType.DMA((22,)),
        pltpu.SemaphoreType.DMA((nc,)),
        pltpu.SemaphoreType.DMA((nc,)),
    ]
    update = pl.pallas_call(
        functools.partial(kernel, nr, nc),
        out_shape=pltpu.VMEM((3, rows, cols), F32),
        in_specs=[hbm] * 10,
        out_specs=vmem,
        scratch_shapes=scratch,
        compiler_params=pltpu.CompilerParams(
            collective_id=0, has_side_effects=True, vmem_limit_bytes=60 * 1024 * 1024
        ),
    )(*args)
    return pl.pallas_call(
        place,
        out_shape=jax.ShapeDtypeStruct((3, rows, cols), F32),
        in_specs=[pl.BlockSpec(memory_space=pltpu.VMEM)],
        out_specs=pl.BlockSpec(memory_space=pl.ANY),
        scratch_shapes=[pltpu.SemaphoreType.DMA((12,))],
        compiler_params=pltpu.CompilerParams(vmem_limit_bytes=1024 * 1024),
    )(update)


def solution(mesh):
    in_specs = (
        P(None, "rows", "cols"),
        P(None, "rows", "cols"),
        P(None, "rows", "cols"),
        P(None, "rows", "cols"),
        P("rows", "cols"),
        P(None, "rows", "cols"),
        P("rows", "cols", None, None),
        P("rows", "cols", None, None),
        P("rows", None),
        P("rows", "cols"),
    )
    out_specs = P(None, "rows", "cols")
    body = functools.partial(shards, mesh.shape["rows"], mesh.shape["cols"])
    return jax.shard_map(body, mesh=mesh, in_specs=in_specs, out_specs=out_specs, check_vma=False)
```

```python
import functools
import math

import jax
import jax.numpy as jnp
from jax import lax
from jax.experimental import pallas as pl
from jax.experimental.pallas import tpu as pltpu
from jax.sharding import PartitionSpec as P

H = 32
PR = 16
PC = 128
L = 128
TOP = 8
MESH = pl.DeviceIdType.MESH
F32 = jnp.float32
BF16 = jnp.bfloat16


def kernel(
    nr, nc,
    res_h, wts_h, acc_h, mob_h, trans_h, cell_h, pinv_h, ci_h, cnt_h, slot_h,
    out_ref,
    res_v, wts_v, acc_v, mob_v, tp_v, cell_v, pinv_v, ci_v, cnt_s, slot_v,
    rp_v, halo_v, ext_v, trow_s, trow_r, tcol_r, drow_s, drow_r, dcol_r, dp_v, cv_v, chr_v, chl_v,
    ps_v, tile_s, tile_r, corr_v,
    load_sem, send_sem, recv_sem, tile_send, tile_recv,
):
    rows = trans_h.shape[0]
    cols = trans_h.shape[1]
    nq = cols // L
    npr = rows // PR
    kmax = ci_h.shape[-1]
    pairs = nq // 2
    order = [pairs - 1] + list(range(pairs - 1))
    me_r = lax.axis_index("rows")
    me_c = lax.axis_index("cols")
    up = lax.rem(me_r + 1, nr)
    down = lax.rem(me_r + nr - 1, nr)
    right = lax.rem(me_c + 1, nc)
    left = lax.rem(me_c + nc - 1, nc)

    def load(src, dst, i):
        copy = pltpu.make_async_copy(src, dst, load_sem.at[i])
        copy.start()
        return copy

    barrier = pltpu.get_barrier_semaphore()
    has_down = me_r > 0
    has_up = me_r < nr - 1
    has_left = me_c > 0
    has_right = me_c < nc - 1
    for target, there in ((up, has_up), (down, has_down)):
        @pl.when(there)
        def _():
            pl.semaphore_signal(barrier, inc=1, device_id=(target, me_c), device_id_type=MESH)

    rw = []
    for n, w in enumerate(order):
        span = pl.ds(w * 2 * L, 2 * L)
        rw.append((
            load(res_h.at[:, :, span], res_v.at[:, :, span], 2 * n),
            load(wts_h.at[:, :, span], wts_v.at[:, :, span], 2 * n + 1),
        ))
        if n == 0:
            load_t = load(trans_h, tp_v.at[pl.ds(TOP, rows), :], 8)
            load_ci = load(ci_h.at[0, 0], ci_v, 9)
            load_slot = load(slot_h, slot_v, 10)
            load_cnt = load(cnt_h, cnt_s, 11)
    for k in range(1, nc):
        pl.semaphore_signal(
            barrier, inc=1, device_id=(me_r, lax.rem(me_c + k, nc)), device_id_type=MESH
        )

    sent = []

    ways = {
        "down": ((down, me_c), has_down, has_up),
        "up": ((up, me_c), has_up, has_down),
        "left": ((me_r, left), has_left, has_right),
        "right": ((me_r, right), has_right, has_left),
    }

    def send(src, dst, i, way):
        device, goes, comes = ways[way]
        copy = pltpu.make_async_remote_copy(
            src_ref=src, dst_ref=dst, send_sem=send_sem.at[i], recv_sem=recv_sem.at[i],
            device_id=device, device_id_type=MESH,
        )
        pl.when(goes)(copy.start)
        sent.append((copy, goes))
        return copy, comes

    def arrive(copies):
        for copy, comes in copies:
            pl.when(comes)(copy.wait_recv)

    body = pl.ds(TOP, rows)
    first = pl.ds(0, L)
    last = pl.ds(cols - L, L)
    halos = []
    for n, w in enumerate(order):
        rw[n][0].wait()
        rw[n][1].wait()
        for q in (2 * w, 2 * w + 1):
            c = slice(q * L, (q + 1) * L)
            for p in range(npr):
                r = slice(p * PR, (p + 1) * PR)
                rp = res_v[0, r, c] * wts_v[0, r, c]
                rp = rp + res_v[1, r, c] * wts_v[1, r, c]
                rp = rp + res_v[2, r, c] * wts_v[2, r, c]
                rp_v[r, c] = rp
                ext_v[H + p * PR : H + (p + 1) * PR, c] = rp.astype(BF16)
                ps_v[p : p + 1, c] = jnp.sum(rp, axis=0, keepdims=True)
        if n == 0:
            pl.semaphore_wait(barrier, nc - 1 + has_down.astype(jnp.int32) + has_up.astype(jnp.int32))
        span = pl.ds(w * 2 * L, 2 * L)
        halos.append((
            send(rp_v.at[pl.ds(0, H), span], halo_v.at[1, :, span], 2 * n, "down"),
            send(rp_v.at[pl.ds(H, H), span], halo_v.at[0, :, span], 2 * n + 1, "up"),
        ))
        if n == 0:
            load_t.wait()
            trow_s[0] = tp_v[TOP : TOP + 1, :]
            trow_s[1] = tp_v[TOP + rows - 1 : TOP + rows, :]
            edge_t = [
                send(tp_v.at[body, first], tcol_r.at[1], 8, "left"),
                send(tp_v.at[body, last], tcol_r.at[0], 9, "right"),
                send(trow_s.at[0], trow_r.at[1], 10, "down"),
                send(trow_s.at[1], trow_r.at[0], 11, "up"),
            ]

    load_p = load(pinv_h.at[0], pinv_v, 12)
    load_m = load(mob_h, mob_v, 13)
    load_a = load(acc_h, acc_v, 14)
    load_c = load(cell_h, cell_v, 15)

    load_ci.wait()
    load_slot.wait()
    lane8 = lax.broadcasted_iota(jnp.int32, (8, L), 1)
    sub8 = lax.broadcasted_iota(jnp.int32, (8, L), 0)
    block = jnp.zeros((kmax, L), F32)
    own = ci_v[...]
    for j in range(kmax):
        block = block + jnp.where(lane8 == me_c * kmax + j, own[:, j : j + 1], 0.0)
    tile_s[0:8, :] = block
    tile_s[8:16, :] = jnp.zeros((8, L), F32)
    lane4 = lax.broadcasted_iota(jnp.int32, (npr, L), 1)
    slots = slot_v[...]
    tiles = jnp.zeros((npr, L), F32)
    hot = []
    for q in range(nq):
        sums = jnp.sum(ps_v[0:npr, q * L : (q + 1) * L], axis=1, keepdims=True)
        hit = lane4 == slots[:, q : q + 1]
        hot.append(hit)
        tiles = tiles + jnp.where(hit, sums, 0.0)
    tiles = jnp.sum(tiles, axis=0, keepdims=True) * (1.0 / math.sqrt(PR * PC))
    tile_s[8:9, :] = tiles
    tile_copies = []
    for k in range(1, nc):
        copy = pltpu.make_async_remote_copy(
            src_ref=tile_s, dst_ref=tile_r.at[k],
            send_sem=tile_send.at[k], recv_sem=tile_recv.at[k],
            device_id=(me_r, lax.rem(me_c + k, nc)), device_id_type=MESH,
        )
        copy.start()
        tile_copies.append(copy)

    for i, row, col in ((0, has_down, has_left), (1, has_up, has_right)):
        @pl.when(jnp.logical_not(row))
        def _():
            drow_r[i] = jnp.zeros(drow_r.shape[1:], F32)

        @pl.when(jnp.logical_not(col))
        def _():
            dcol_r[i] = jnp.zeros(dcol_r.shape[1:], F32)

    arrive(edge_t)
    tp_v[TOP - 1 : TOP, :] = trow_r[0]
    tp_v[TOP + rows : TOP + rows + 1, :] = trow_r[1]

    lane16 = lax.broadcasted_iota(jnp.int32, (PR, L), 1)
    is_last = lane16 == L - 1
    is_first = lane16 == 0

    def mean(a, b):
        return 2.0 * a * b / (a + b)

    for q in range(nq):
        c = slice(q * L, (q + 1) * L)
        low = mean(tp_v[TOP - 1 : TOP, c], tp_v[TOP : TOP + 1, c])
        cv_v[TOP - 1 : TOP, c] = jnp.where(me_r > 0, low, 0.0)
    for p in range(npr):
        r0 = TOP + p * PR
        r = slice(p * PR, (p + 1) * PR)
        blocks = [tcol_r[0, r, :]]
        blocks += [tp_v[r0 : r0 + PR, q * L : (q + 1) * L] for q in range(nq)]
        blocks += [tcol_r[1, r, :]]
        turned = [pltpu.roll(b, L - 1, 1) for b in blocks[1:]]
        before = None
        for q in range(nq + 1):
            here = blocks[q]
            if q == 0:
                near = turned[0]
            else:
                near = jnp.where(is_last, turned[q], turned[q - 1])
            face = mean(here, near)
            if q == 0:
                face = jnp.where(me_c > 0, face, 0.0)
            if q == nq:
                face = jnp.where(is_last & (me_c == nc - 1), 0.0, face)
            moved = pltpu.roll(face, 1, 1)
            if q > 0:
                c = slice((q - 1) * L, q * L)
                chr_v[r, c] = face
                chl_v[r, c] = jnp.where(is_first, before, moved)
                cv_v[r0 : r0 + PR, c] = mean(here, tp_v[r0 + 1 : r0 + PR + 1, c])
            before = moved
    for q in range(nq):
        c = slice(q * L, (q + 1) * L)
        r = slice(TOP + rows - 1, TOP + rows)
        cv_v[r, c] = jnp.where(me_r < nr - 1, cv_v[r, c], 0.0)

    load_p.wait()
    load_cnt.wait()
    row_e = lax.broadcasted_iota(jnp.int32, (H, L), 0)
    lo_count = jnp.where(me_r > 0, cnt_s[0, 0], 0)
    hi_count = jnp.where(me_r < nr - 1, cnt_s[0, 1], 0)

    for copy in tile_copies:
        copy.wait_recv()
    total = tile_s[8:16, :]
    for k in range(1, nc):
        total = total + tile_r[k, 8:16, :]
    total = total[0:1, :]
    coarse = jnp.zeros((8, L), F32)
    for k in range(nc):
        part = tile_s[0:8, :] if k == 0 else tile_r[k, 0:8, :]
        owner = lax.rem(me_c - k + nc, nc)
        value = jnp.sum(part * total, axis=1, keepdims=True)
        coarse = coarse + jnp.where(lane8 == owner * kmax + sub8, value, 0.0)
    coarse = jnp.sum(coarse, axis=0, keepdims=True)
    for q in range(nq):
        corr = jnp.sum(jnp.where(hot[q], coarse, 0.0), axis=1, keepdims=True)
        corr_v[0:npr, q * L : (q + 1) * L] = jnp.broadcast_to(corr, (npr, L))

    def column(p, q):
        r0 = TOP + p * PR
        if q < 0:
            return dcol_r[0, p * PR : (p + 1) * PR, :]
        if q == nq:
            return dcol_r[1, p * PR : (p + 1) * PR, :]
        return dp_v[r0 : r0 + PR, q * L : (q + 1) * L]

    def finish(p, q):
        r0 = TOP + p * PR
        r = slice(p * PR, (p + 1) * PR)
        c = slice(q * L, (q + 1) * L)
        here = column(p, q)
        after = jnp.where(is_last, pltpu.roll(column(p, q + 1), L - 1, 1), pltpu.roll(here, L - 1, 1))
        prior = jnp.where(is_first, pltpu.roll(column(p, q - 1), 1, 1), pltpu.roll(here, 1, 1))
        flux = chr_v[r, c] * (here - after) + chl_v[r, c] * (here - prior)
        flux = flux + cv_v[r0 : r0 + PR, c] * (here - dp_v[r0 + 1 : r0 + PR + 1, c])
        flux = flux + cv_v[r0 - 1 : r0 + PR - 1, c] * (here - dp_v[r0 - 1 : r0 + PR - 1, c])
        r2 = [
            res_v[k, r, c]
            - (acc_v[k, r, c].astype(F32) * here + mob_v[k, r, c].astype(F32) * flux)
            for k in range(3)
        ]
        for k in range(3):
            u = cell_v[3 * k, r, c].astype(F32) * r2[0]
            u = u + cell_v[3 * k + 1, r, c].astype(F32) * r2[1]
            u = u + cell_v[3 * k + 2, r, c].astype(F32) * r2[2]
            if k == 0:
                u = u + here
            out_ref[k, r, c] = u

    edge_c = []
    edge_r = []
    for n, w in enumerate(order):
        arrive(halos[n])
        for q in (2 * w, 2 * w + 1):
            c = slice(q * L, (q + 1) * L)
            low = jnp.where(row_e >= H - lo_count, halo_v[0, :, c], 0.0)
            high = jnp.where(row_e < hi_count, halo_v[1, :, c], 0.0)
            ext_v[0:H, c] = low.astype(BF16)
            ext_v[H + rows : 2 * H + rows, c] = high.astype(BF16)
            z = jnp.dot(pinv_v[q, H : H + rows, :], ext_v[:, c], preferred_element_type=F32)
            for p in range(npr):
                dp = z[p * PR : (p + 1) * PR, :] + corr_v[p : p + 1, c]
                dp_v[TOP + p * PR : TOP + (p + 1) * PR, c] = dp
                if p == 0:
                    drow_s[0, :, c] = dp[0:1, :]
                    dp_v[TOP - 1 : TOP, c] = dp[0:1, :]
                if p == npr - 1:
                    drow_s[1, :, c] = dp[PR - 1 : PR, :]
                    dp_v[TOP + rows : TOP + rows + 1, c] = dp[PR - 1 : PR, :]
        span = pl.ds(w * 2 * L, 2 * L)
        edge_r.append(send(drow_s.at[0, :, span], drow_r.at[1, :, span], 12 + 2 * n, "down"))
        edge_r.append(send(drow_s.at[1, :, span], drow_r.at[0, :, span], 13 + 2 * n, "up"))
        if w == pairs - 1:
            edge_c.append(send(dp_v.at[body, last], dcol_r.at[0], 20, "right"))
        if w == 0:
            edge_c.append(send(dp_v.at[body, first], dcol_r.at[1], 21, "left"))
        if n == pairs - 2:
            load_m.wait()
            load_a.wait()
            load_c.wait()
            for q in range(1, nq - 5):
                for p in range(npr):
                    finish(p, q)

    for q in range(nq - 5, nq - 1):
        for p in range(npr):
            finish(p, q)
    arrive(edge_c)
    for q in (0, nq - 1):
        for p in range(npr):
            finish(p, q)
    arrive(edge_r)
    for q in range(nq):
        c = slice(q * L, (q + 1) * L)
        for e in range(2):
            r = slice(0, 8) if e == 0 else slice(rows - 8, rows)
            face = slice(TOP - 1, TOP) if e == 0 else slice(TOP + rows - 1, TOP + rows)
            mine = slice(TOP, TOP + 1) if e == 0 else slice(TOP + rows - 1, TOP + rows)
            extra = cv_v[face, c] * (dp_v[mine, c] - drow_r[e, :, c])
            extra = jnp.where(sub8 == (0 if e == 0 else 7), extra, 0.0)
            m = [mob_v[j, r, c].astype(F32) * extra for j in range(3)]
            for k in range(3):
                u = cell_v[3 * k, r, c].astype(F32) * m[0]
                u = u + cell_v[3 * k + 1, r, c].astype(F32) * m[1]
                u = u + cell_v[3 * k + 2, r, c].astype(F32) * m[2]
                out_ref[k, r, c] = out_ref[k, r, c] - u
    for copy, goes in sent:
        pl.when(goes)(copy.wait_send)
    for copy in tile_copies:
        copy.wait_send()


def place(in_ref, out_ref, sem):
    copy = pltpu.make_async_copy(in_ref, out_ref, sem.at[0])
    copy.start()
    copy.wait()


def shards(nr, nc, *args):
    residual, pinv = args[0], args[6]
    rows, cols = residual.shape[1:]
    groups = pinv.shape[1]
    e = rows + 2 * H
    hbm = pl.BlockSpec(memory_space=pl.ANY)
    vmem = pl.BlockSpec(memory_space=pltpu.VMEM)
    tall = rows + 2 * TOP
    scratch = [
        pltpu.VMEM((3, rows, cols), F32),
        pltpu.VMEM((3, rows, cols), F32),
        pltpu.VMEM((3, rows, cols), BF16),
        pltpu.VMEM((3, rows, cols), BF16),
        pltpu.VMEM((tall, cols), F32),
        pltpu.VMEM((9, rows, cols), BF16),
        pltpu.VMEM((groups, e, L), BF16),
        pltpu.VMEM(args[7].shape[2:], F32),
        pltpu.SMEM(args[8].shape, jnp.int32),
        pltpu.VMEM(args[9].shape, jnp.int32),
        pltpu.VMEM((rows, cols), F32),
        pltpu.VMEM((2, H, cols), F32),
        pltpu.VMEM((e, cols), BF16),
        pltpu.VMEM((2, 1, cols), F32),
        pltpu.VMEM((2, 1, cols), F32),
        pltpu.VMEM((2, rows, L), F32),
        pltpu.VMEM((2, 1, cols), F32),
        pltpu.VMEM((2, 1, cols), F32),
        pltpu.VMEM((2, rows, L), F32),
        pltpu.VMEM((tall, cols), F32),
        pltpu.VMEM((tall, cols), F32),
        pltpu.VMEM((rows, cols), F32),
        pltpu.VMEM((rows, cols), F32),
        pltpu.VMEM((8, cols), F32),
        pltpu.VMEM((16, L), F32),
        pltpu.VMEM((nc, 16, L), F32),
        pltpu.VMEM((8, cols), F32),
        pltpu.SemaphoreType.DMA((16,)),
        pltpu.SemaphoreType.DMA((22,)),
        pltpu.SemaphoreType.DMA((22,)),
        pltpu.SemaphoreType.DMA((nc,)),
        pltpu.SemaphoreType.DMA((nc,)),
    ]
    update = pl.pallas_call(
        functools.partial(kernel, nr, nc),
        out_shape=pltpu.VMEM((3, rows, cols), F32),
        in_specs=[hbm] * 10,
        out_specs=vmem,
        scratch_shapes=scratch,
        compiler_params=pltpu.CompilerParams(
            collective_id=0, has_side_effects=True, vmem_limit_bytes=60 * 1024 * 1024
        ),
    )(*args)
    return pl.pallas_call(
        place,
        out_shape=jax.ShapeDtypeStruct((3, rows, cols), F32),
        in_specs=[pl.BlockSpec(memory_space=pltpu.VMEM)],
        out_specs=pl.BlockSpec(memory_space=pl.ANY),
        scratch_shapes=[pltpu.SemaphoreType.DMA((1,))],
        compiler_params=pltpu.CompilerParams(vmem_limit_bytes=1024 * 1024),
    )(update)


def solution(mesh):
    in_specs = (
        P(None, "rows", "cols"),
        P(None, "rows", "cols"),
        P(None, "rows", "cols"),
        P(None, "rows", "cols"),
        P("rows", "cols"),
        P(None, "rows", "cols"),
        P("rows", "cols", None, None),
        P("rows", "cols", None, None),
        P("rows", None),
        P("rows", "cols"),
    )
    out_specs = P(None, "rows", "cols")
    body = functools.partial(shards, mesh.shape["rows"], mesh.shape["cols"])
    return jax.shard_map(body, mesh=mesh, in_specs=in_specs, out_specs=out_specs, check_vma=False)
```
